32 devices in a mesh: grp: 2 (over x), tpl: 16 (over z, y, core).
Axes of the slice: x: 2, y: 2, z: 4, core: 2. Of those that a mesh axis runs over, the one named last changes fastest.
Arguments:
- strain_slots: bfloat16 [32, 3, 2, 262144], P(('grp', 'tpl')), parts along dimension 0, may hold values from -6 to 6
- templates: bfloat16 [32, 2, 262144], P(None, None, 'tpl'), may hold values from -6 to 6
- cutoffs: int32 [32], replicated, may hold values from 32768 to 262144
- lists: int32 [16, 2], replicated, may hold values from 0 to 31, as said below
- owner: int32 [2], P('grp'), parts along dimension 0, may hold values from 0 to 15
- slides: int32 [6], P('grp'), parts along dimension 0, may hold values from 0 to 262143
Outputs:
- peaks: float32 [64], P(('grp', 'tpl')), parts along dimension 0
- norms: float32 [64], P(('grp', 'tpl')), parts along dimension 0
The draws below stay inside these ranges and needn't reach their ends.
There are 2 independent parts, one for each index of `grp`. The reference program is written for one: setup_inputs(seed, part) draws one part's arguments, and reference() takes and returns one part's arrays. A program takes and returns all parts, laid end to end along the dimension named above; an argument that names none is the same for every part. Nothing has to cross between parts.
Inputs may be any that keep to these rules, and one draw needn't show every extreme that they name: Every template appears once in lists; list positions in row-major order run through the templates by falling cutoffs. One template has cutoff 262144, one has 32768.
All inputs are finite; a program needn't handle non-finite values.
Results may differ from the reference program's by a relative error of at most 0.0021.
Values may be sent and summed in bfloat16 or wider, within the bound.
A program may use at most 128 MiB of HBM per device.

```python
import jax
import jax.numpy as jnp
from jax import lax

DET = 3
ROWS = 512
COLS = 512
TPL_DEV = 2
BINS = 262144
TEMPLATES = 32
SLOTS = 16
N_TPL = 16


def bank_draw(key):
    keys = jax.random.split(jax.random.fold_in(key, 7), 3)
    cutoff_bins = jax.random.randint(keys[0], (TEMPLATES,), BINS // 8, BINS + 1)
    marks = jax.random.permutation(keys[1], TEMPLATES)
    cutoff_bins = jnp.where(marks == 0, BINS, cutoff_bins)
    cutoff_bins = jnp.where(marks == 1, BINS // 8, cutoff_bins)
    breakers = jax.random.permutation(keys[2], TEMPLATES)
    scores = cutoff_bins * TEMPLATES + breakers
    ordered = jnp.argsort(-scores, stable=True)
    return (cutoff_bins.astype(jnp.int32), ordered.astype(jnp.int32).reshape(TEMPLATES // TPL_DEV, TPL_DEV))


def draw_cutoffs(key, part):
    return bank_draw(key)[0]


def draw_lists(key, part):
    return bank_draw(key)[1]


def level_of(rng, shape, cuts, least, largest):
    factor_of, own = 1.0, jax.random.fold_in(rng, 6)
    for axis_at, parts in cuts:
        draws = jnp.exp(jax.random.uniform(jax.random.fold_in(own, axis_at), (parts,), jnp.float32, least / len(cuts), largest / len(cuts)))
        factor_of = factor_of * jnp.repeat(draws, shape[axis_at] // parts).reshape([-1 if axis == axis_at else 1 for axis in range(len(shape))])
    return factor_of


def normal_values(key, shape, scale, bound, shards=(), held_as=jnp.bfloat16):
    level = level_of(key, shape, shards, -0.22, 0.18) if shards else 1.0
    result = jax.random.normal(key, shape, jnp.float32) * scale * level
    return jnp.minimum(jnp.maximum(result, -bound), bound).astype(held_as)


def setup_inputs(seed: int = 0, part: int = 0) -> dict:
    key_list = jax.random.split(jax.random.key(seed), 7)
    part_splits = jax.random.split(jax.random.fold_in(key_list[6], part), 7)
    return {
        "strain_slots": normal_values(part_splits[0], (SLOTS, DET, 2, BINS), 1.0, 6.0, ((0, 16),)),
        "templates": normal_values(key_list[1], (TEMPLATES, 2, BINS), 1.0, 6.0, ((2, 16),)),
        "cutoffs": draw_cutoffs(jax.random.fold_in(key_list[6], 71), part),
        "lists": draw_lists(jax.random.fold_in(key_list[6], 71), part),
        "owner": jax.random.randint(part_splits[4], (1,), 0, N_TPL).astype(jnp.int32),
        "slides": jax.random.randint(part_splits[5], (DET,), 0, BINS).astype(jnp.int32),
    }


two_pi = 6.283185307179586
eps_norm = 1e-6


def turn_table(left_ids, right_ids, period):
    product_idx = (left_ids[:, None] * right_ids[None, :]) % period
    angles = product_idx.astype(jnp.float32) * (two_pi / period)
    return jnp.cos(angles), jnp.sin(angles)


def slide_phases(slides):
    total = ROWS * COLS
    bin_ids = jnp.arange(total, dtype=jnp.int32)
    row_ids = bin_ids // COLS
    col_ids = bin_ids % COLS
    stride = (COLS * slides) % total
    turns = ((row_ids[None, :] * stride[:, None]) % total + (col_ids[None, :] * slides[:, None]) % total) % total
    angles = turns.astype(jnp.float32) * (two_pi / total)
    return jnp.cos(angles), jnp.sin(angles)


def rounded(values):
    return lax.optimization_barrier(values.astype(jnp.bfloat16)).astype(jnp.float32)


def reference(strain_slots, templates, cutoffs, lists, owner, slides):
    total = ROWS * COLS
    strain = lax.dynamic_index_in_dim(strain_slots, owner[0], 0, keepdims=False).astype(jnp.float32)
    row_ids = jnp.arange(ROWS, dtype=jnp.int32)
    col_ids = jnp.arange(COLS, dtype=jnp.int32)
    row_cos, row_sin = turn_table(row_ids, row_ids, ROWS)
    row_table = rounded(jnp.concatenate([jnp.concatenate([row_cos, -row_sin], 1), jnp.concatenate([row_sin, row_cos], 1)], 0))
    twiddle_cos, twiddle_sin = turn_table(row_ids, col_ids, total)
    col_cos, col_sin = turn_table(col_ids, col_ids, COLS)
    col_table = rounded(jnp.concatenate([jnp.concatenate([col_cos, col_sin], 1), jnp.concatenate([-col_sin, col_cos], 1)], 0))
    phase_cos, phase_sin = slide_phases(slides)
    data_re = strain[:, 0]
    data_im = strain[:, 1]

    def filter_one(template_id):
        waveform = lax.dynamic_index_in_dim(templates, template_id, 0, keepdims=False).astype(jnp.float32)
        cutoff = lax.dynamic_index_in_dim(cutoffs, template_id, 0, keepdims=False)
        inside = jnp.arange(total, dtype=jnp.int32) < cutoff
        wave_re = waveform[0]
        wave_im = waveform[1]
        real_part = data_re * wave_re + data_im * wave_im
        imag_part = data_im * wave_re - data_re * wave_im
        prod_re = jnp.where(inside, real_part * phase_cos - imag_part * phase_sin, jnp.float32(0.0))
        prod_im = jnp.where(inside, real_part * phase_sin + imag_part * phase_cos, jnp.float32(0.0))
        stacked = rounded(jnp.concatenate([prod_re.reshape(DET, ROWS, COLS), prod_im.reshape(DET, ROWS, COLS)], 1))
        section_one = jnp.einsum("ab,dbc->dac", row_table, stacked, precision=lax.Precision.HIGHEST)
        first_re = section_one[:, :ROWS]
        first_im = section_one[:, ROWS:]
        twisted = rounded(jnp.concatenate([first_re * twiddle_cos - first_im * twiddle_sin, first_re * twiddle_sin + first_im * twiddle_cos], 2))
        series = jnp.einsum("dab,bc->dac", twisted, col_table, precision=lax.Precision.HIGHEST)
        series_re = series[:, :, :COLS]
        series_im = series[:, :, COLS:]
        power_sum = jnp.sum(series_re * series_re + series_im * series_im, axis=0)
        sigmasq = jnp.sum(jnp.where(inside, wave_re * wave_re + wave_im * wave_im, jnp.float32(0.0)))
        return jnp.max(power_sum) / (2.0 * (sigmasq + eps_norm)), sigmasq / total

    peaks, norms = lax.map(filter_one, lists.reshape(-1).astype(jnp.int32))
    return peaks, norms
```

```python
import functools

import jax
import jax.numpy as jnp
import numpy as np
from jax import lax
from jax.experimental import pallas as pl
from jax.experimental.pallas import tpu as pltpu
from jax.sharding import PartitionSpec as P

ROWS = 512
COLS = 512
RADIX = 4
FOLD = ROWS // RADIX
WIDE = RADIX * COLS
HALF = COLS // 2
LANES = 128
CHUNKS = WIDE // LANES
TALL = 2 * FOLD * CHUNKS

two_pi = 6.283185307179586
eps_norm = 1e-06

MESH = pl.DeviceIdType.MESH
LEAD = 2
LAG = 2
CROSS_LAG = 3


def turn_table(left_ids, right_ids, period):
    product_idx = left_ids[:, None] * right_ids[None, :] % period
    angles = product_idx.astype(np.float32) * np.float32(two_pi / period)
    return np.cos(angles), np.sin(angles)


def constant_tables():
    ids = np.arange(ROWS, dtype=np.int32)
    cos, sin = turn_table(ids[:FOLD], ids, ROWS)
    first = []
    for r in range(RADIX):
        c, s = cos[:, r::RADIX], sin[:, r::RADIX]
        first.append(np.concatenate([np.concatenate([c, -s], 1), np.concatenate([s, c], 1)], 0))
    twiddle = np.stack(turn_table(ids, ids, ROWS * COLS))
    cos, sin = turn_table(ids, ids[: HALF + 1], COLS)
    sin = sin[:, :HALF].copy()
    sin[:, 0] = cos[:, HALF]
    second = np.concatenate([cos[:, :HALF], sin], 1)
    return np.stack(first).astype(jnp.bfloat16), twiddle, second.astype(jnp.bfloat16)


def send_order(depth):
    orders = []
    for z in range(depth):
        need = [(depth - 1 - j + z if j > z else j + depth - 1 - z if j < z else depth, j) for j in range(depth)]
        orders.append([j for _, j in sorted(need)])
    return orders


def kernel(
    width, lists, owner, cutoffs, slides, strain, bank_hbm, first_hbm, twiddle_hbm, second_hbm,
    peaks, norms,
    mine, other, ysend, yrecv, zin, full, bank, picked, arrived, flat, row_phase, col_phase,
    turned, masked, twisted, total_q, total_r, first, twiddle, second,
    local_sem, core_send, core_recv, y_send, y_recv, z_send, z_recv, ag_send, ag_recv,
    yag_send, yag_recv, part_send, part_recv, swap_send, swap_recv, cross_send, cross_recv,
):
    n, groups = lax.axis_size("tpl"), lax.axis_size("grp")
    me, group = lax.axis_index("tpl"), lax.axis_index("grp")
    depth = n // 2 // width
    core, chip = me % 2, me // 2
    y, z = chip % width, chip // width
    dets = strain.shape[0]
    half = strain.shape[1] // 2
    prow = half // (width * depth)
    slots = lists.shape[0]
    shard = bank.shape[1]
    hrow = shard // groups
    partner = me + 1 - 2 * core

    def device(yy, zz):
        return (zz * width + yy) * 2 + core

    across = device(width - 1 - y, z)
    onward = (device(y, jnp.minimum(z + 1, depth - 1)), device(y, jnp.maximum(z - 1, 0)))

    own_id = owner[0]
    own_chip = own_id // 2
    i_own = own_id == me
    chip_owns = own_chip == chip
    line_owns = own_chip // width == z
    from_left = own_chip // width < z

    def remote(src, dst, send, recv, **where):
        return pltpu.make_async_remote_copy(
            src_ref=src, dst_ref=dst, send_sem=send, recv_sem=recv, device_id=where, device_id_type=MESH
        )

    def rows(base, size):
        return pl.ds(pl.multiple_of(base, 16), size)

    def place(yy, j):
        return rows((yy * depth + j) * prow, prow)

    def spot(cc, yy, j):
        return rows(cc * half + (yy * depth + j) * prow, prow)

    def core_copy(s, yy, j):
        k = yy * depth + j
        return remote(
            strain.at[s, spot(1 - core, yy, j)], other.at[s, place(yy, j)],
            core_send.at[s, k], core_recv.at[s, k], tpl=partner,
        )

    def y_copy(s, j):
        return remote(ysend.at[s, j], yrecv.at[s, j], y_send.at[s, j], y_recv.at[s, j], tpl=across)

    def z_copy(way, s, j):
        at = zin.at[way, s, j]
        return remote(at, at, z_send.at[way, s, j], z_recv.at[way, s, j], tpl=onward[way])

    def ag_copy(way, s, j):
        at = full.at[s, spot(core, y, j)]
        return remote(at, at, ag_send.at[way, s, j], ag_recv.at[way, s, j], tpl=onward[way])

    def yag_copy(s, j):
        at = full.at[s, spot(core, y, j)]
        return remote(at, at, yag_send.at[s, j], yag_recv.at[s, j], tpl=across)

    def part_copy(s, cc, yy, j):
        at = full.at[s, spot(cc, yy, j)]
        k = yy * depth + j
        return remote(at, at, part_send.at[s, k], part_recv.at[s, k], tpl=partner)

    def swap_copy(slot, i):
        to = (me - i + n) % n
        return remote(
            picked.at[slot, to], arrived.at[slot, me, rows(group * hrow, hrow)],
            swap_send.at[slot, i], swap_recv.at[slot, i], tpl=to,
        )

    def swap_arrival(slot, i):
        source = (me + i) % n
        return remote(
            picked.at[slot, me], arrived.at[slot, source, rows(group * hrow, hrow)],
            swap_send.at[slot, i], swap_recv.at[slot, i], tpl=source,
        )

    def cross_copy(slot, i, g):
        at = arrived.at[slot, (me + i) % n, rows(group * hrow, hrow)]
        return remote(
            at, at, cross_send.at[slot, g - 1, i], cross_recv.at[slot, g - 1, i], grp=(group + g) % groups
        )

    def cross_arrival(slot, i, g):
        source = (group - g + groups) % groups
        at = arrived.at[slot, (me + i) % n, rows(source * hrow, hrow)]
        return remote(at, at, cross_send.at[slot, g - 1, i], cross_recv.at[slot, g - 1, i], grp=source)

    locals_ = [
        pltpu.make_async_copy(strain.at[:, rows(core * half, half)], mine, local_sem.at[0]),
        pltpu.make_async_copy(bank_hbm, bank, local_sem.at[1]),
        pltpu.make_async_copy(first_hbm, first, local_sem.at[2]),
        pltpu.make_async_copy(twiddle_hbm, twiddle, local_sem.at[3]),
        pltpu.make_async_copy(second_hbm, second, local_sem.at[4]),
    ]
    for copy in locals_[:2]:
        copy.start()

    barrier = pltpu.get_barrier_semaphore()

    def greet(i, _):
        pl.semaphore_signal(barrier, inc=1, device_id={"tpl": (me + i) % n}, device_id_type=MESH)
        return 0

    lax.fori_loop(1, n, greet, 0)
    for g in range(1, groups):
        pl.semaphore_signal(barrier, inc=1, device_id={"grp": (group + g) % groups}, device_id_type=MESH)
    pl.semaphore_wait(barrier, n - 1 + groups - 1)

    orders = send_order(depth)

    def ordered(o):
        j = 0
        for zz in range(depth):
            j = jnp.where(z == zz, orders[zz][o], j)
        return j

    def start_core(s):
        for o in range(depth):
            for yy in (width - 1 - y, y)[2 - width:]:
                core_copy(s, yy, ordered(o)).start()

    def candidate(s, yy, j):
        return jnp.where(i_own, mine[s, place(yy, j)], other[s, place(yy, j)])

    def open_det(s):
        if width == 1:
            return
        for o in range(depth):
            j = ordered(o)
            core_copy(s, 1 - y, j).wait_recv()
            ysend[s, j] = candidate(s, 1 - y, j)
            y_copy(s, j).start()

    def merged(s, j):
        core_copy(s, y, j).wait_recv()
        got = candidate(s, y, j)
        if width == 1:
            return got
        y_copy(s, j).wait_recv()
        return jnp.where(chip_owns, got, yrecv[s, j])

    def pass_on(s, j):
        if width > 1:
            yag_copy(s, j).start()
        part_copy(s, core, y, j).start()

    def reduce_step(s, step):
        for way in range(2):
            behind = z if way == 0 else depth - 1 - z
            j = depth - 1 - step + z if way == 0 else step - (depth - 1 - z)

            @pl.when((step >= behind) & (step < depth - 1))
            def _():
                value = merged(s, j)

                @pl.when(behind == 0)
                def _():
                    zin[way, s, j] = value

                @pl.when(behind > 0)
                def _():
                    z_copy(way, s, j).wait_recv()
                    zin[way, s, j] = jnp.where(line_owns, value, zin[way, s, j])

                z_copy(way, s, j).start()

        @pl.when(step == depth - 1)
        def _():
            value = merged(s, z)

            @pl.when(z > 0)
            def _():
                z_copy(0, s, z).wait_recv()

            @pl.when(z < depth - 1)
            def _():
                z_copy(1, s, z).wait_recv()

            @pl.when(z == 0)
            def _():
                full[s, spot(core, y, z)] = jnp.where(line_owns, value, zin[1, s, z])

            @pl.when(z == depth - 1)
            def _():
                full[s, spot(core, y, z)] = jnp.where(line_owns, value, zin[0, s, z])

            @pl.when((z > 0) & (z < depth - 1))
            def _():
                full[s, spot(core, y, z)] = jnp.where(
                    line_owns, value, jnp.where(from_left, zin[0, s, z], zin[1, s, z])
                )

            @pl.when(z < depth - 1)
            def _():
                ag_copy(0, s, z).start()

            @pl.when(z > 0)
            def _():
                ag_copy(1, s, z).start()

            pass_on(s, z)

    def gather_step(s, h):
        for way in range(2):
            j = z - h if way == 0 else z + h
            ahead = depth - 1 - z if way == 0 else z

            @pl.when((h >= 1) & (h < depth) & (j >= 0) & (j < depth))
            def _():
                ag_copy(way, s, j).wait_recv()

                @pl.when(ahead > 0)
                def _():
                    ag_copy(way, s, j).start()

                pass_on(s, j)

    def hand_step(s, h):
        if width == 1:
            return
        for way in range(2):
            j = z - h if way == 0 else z + h

            @pl.when((h >= way) & (h < depth) & (j >= 0) & (j < depth))
            def _():
                at = full.at[s, spot(core, 1 - y, j)]
                remote(at, at, yag_send.at[s, j], yag_recv.at[s, j], tpl=across).wait_recv()
                part_copy(s, core, 1 - y, j).start()

    for s in range(dets):
        start_core(s)
    locals_[0].wait()
    open_det(0)
    for copy in locals_[2:]:
        copy.start()
    locals_[1].wait()

    def pick(d, _):
        for slot in range(slots):
            picked[slot, d] = bank[lists[slot, d], rows(group * hrow, hrow)]
        return 0

    lax.fori_loop(0, n, pick, 0)
    for slot in range(slots):
        arrived[slot, me] = bank[lists[slot, me]]

    steps = LEAD * (dets - 1) + 2 * (depth - 1) + LAG + 1
    messages = slots * (n - 1)
    per_step = -(-messages // (steps - CROSS_LAG))

    def swap_start(q):
        swap_copy(q // (n - 1), 1 + q % (n - 1)).start()

    def cross_start(q):
        slot, i = q // (n - 1), 1 + q % (n - 1)
        swap_arrival(slot, i).wait_recv()
        for g in range(1, groups):
            cross_copy(slot, i, g).start()

    def step_body(t, _):
        for s in range(dets):
            if s > 0:
                @pl.when(t == LEAD * s - 1)
                def _():
                    open_det(s)
            reduce_step(s, t - LEAD * s)
            gather_step(s, t - LEAD * s - (depth - 1))
            hand_step(s, t - LEAD * s - (depth - 1) - LAG)
        for e in range(per_step):
            q = t * per_step + e

            @pl.when(q < messages)
            def _():
                swap_start(q)

            p = (t - CROSS_LAG) * per_step + e

            @pl.when((p >= 0) & (p < messages))
            def _():
                cross_start(p)
        return 0

    lax.fori_loop(0, steps, step_body, 0)

    def drain(j, _):
        for s in range(dets):
            for yy in range(width):
                core_copy(s, yy, j).wait_send()
                part_copy(s, core, yy, j).wait_send()
                part_copy(s, 1 - core, yy, j).wait_recv()
            if width > 1:
                y_copy(s, j).wait_send()
                yag_copy(s, j).wait_send()
            for way in range(2):
                ahead = depth - 1 - z if way == 0 else z
                passes = j > z if way == 0 else j < z

                @pl.when((ahead > 0) & passes)
                def _():
                    z_copy(way, s, j).wait_send()

                @pl.when((ahead > 0) & jnp.logical_not(passes))
                def _():
                    ag_copy(way, s, j).wait_send()
        return 0

    lax.fori_loop(0, depth, drain, 0)

    def finish_swap(i, _):
        for slot in range(slots):
            swap_copy(slot, i).wait_send()
            for g in range(1, groups):
                cross_copy(slot, i, g).wait_send()
                cross_arrival(slot, i, g).wait_recv()
        return 0

    lax.fori_loop(1, n, finish_swap, 0)
    for copy in locals_[2:]:
        copy.wait()

    make_phases(slides, row_phase, col_phase)
    for d in range(dets):
        turn_det(full.at[d], flat, row_phase.at[d], col_phase.at[d], turned.at[d])
    for slot in range(slots):
        cutoff = cutoffs[lists[slot, me]]
        sigmasq = mask_template(cutoff, arrived.at[slot], flat, masked)
        peak = filter_template(turned, masked, first, twiddle, second, twisted, total_q, total_r)
        peaks[slot] = peak / (2.0 * (sigmasq + eps_norm))
        norms[slot] = sigmasq / (ROWS * COLS)


def make_phases(slides, row_phase, col_phase):
    total = ROWS * COLS
    for d in range(row_phase.shape[0]):
        slide = slides[d]
        row = lax.broadcasted_iota(jnp.int32, (FOLD, LANES), 0) * slide % FOLD
        row = row.astype(jnp.float32) * (two_pi / FOLD)
        row_phase[d, 0] = jnp.cos(row)
        row_phase[d, 1] = jnp.sin(row)
        col = lax.broadcasted_iota(jnp.int32, (8, WIDE), 1) * slide % total
        col = col.astype(jnp.float32) * (two_pi / total)
        col_phase[d, 0] = jnp.cos(col)
        col_phase[d, 1] = jnp.sin(col)


def widen(source, flat):
    size = 256

    def body(i, _):
        at = pl.ds(pl.multiple_of(i * size, size), size)
        flat[at, :] = source[at, :].astype(jnp.float32)
        return 0

    lax.fori_loop(0, TALL // size, body, 0)


def tile(flat, i, c, part):
    return flat[pl.ds((i * 8 * CHUNKS + c) * 2 + part, 8, stride=2 * CHUNKS), :]


def turn_det(source, flat, row_phase, col_phase, turned):
    widen(source, flat)

    def body(i, _):
        at = pl.ds(pl.multiple_of(i * 8, 8), 8)
        rr, ri = row_phase[0, at, :], row_phase[1, at, :]
        for c in range(CHUNKS):
            cols = pl.ds(c * LANES, LANES)
            cr, ci = col_phase[0, :, cols], col_phase[1, :, cols]
            pr, pi = rr * cr - ri * ci, rr * ci + ri * cr
            xr, xi = tile(flat, i, c, 0), tile(flat, i, c, 1)
            turned[0, at, cols] = xr * pr - xi * pi
            turned[1, at, cols] = xr * pi + xi * pr
        return 0

    lax.fori_loop(0, FOLD // 8, body, 0)


def mask_template(cutoff, source, flat, masked):
    shards, shard = source.shape[0], source.shape[1]

    def body(i, _):
        flat[pl.ds(pl.multiple_of(i * shard, shard), shard), :] = source[i].astype(jnp.float32)
        return 0

    lax.fori_loop(0, shards, body, 0)

    def mask(i, acc):
        at = pl.ds(pl.multiple_of(i * 8, 8), 8)
        base = (lax.broadcasted_iota(jnp.int32, (8, LANES), 0) + i * 8) * WIDE + lax.broadcasted_iota(
            jnp.int32, (8, LANES), 1
        )
        for c in range(CHUNKS):
            cols = pl.ds(c * LANES, LANES)
            inside = base < cutoff - c * LANES
            wr = jnp.where(inside, tile(flat, i, c, 0), 0.0)
            wi = jnp.where(inside, tile(flat, i, c, 1), 0.0)
            masked[0, at, cols] = wr
            masked[1, at, cols] = wi
            acc = acc + (wr * wr + wi * wi)
        return acc

    return jnp.sum(lax.fori_loop(0, FOLD // 8, mask, jnp.zeros((8, LANES), jnp.float32)))


def filter_template(turned, masked, first, twiddle, second, twisted, total_q, total_r):
    dets = turned.shape[0]

    def one_detector(d, _):
        for c in range(COLS // 256):
            parts = []
            for r in range(RADIX):
                cols = pl.ds(r * COLS + c * 256, 256)
                xr, xi = turned[d, 0, :, cols], turned[d, 1, :, cols]
                wr, wi = masked[0, :, cols], masked[1, :, cols]
                product = jnp.concatenate([xr * wr + xi * wi, xi * wr - xr * wi], 0)
                out = jnp.dot(first[r], product.astype(jnp.bfloat16), preferred_element_type=jnp.float32)
                parts.append((out[:FOLD], out[FOLD:]))
            (r0, i0), (r1, i1), (r2, i2), (r3, i3) = parts
            ar, ai, br, bi = r0 + r2, i0 + i2, r0 - r2, i0 - i2
            cr, ci, dr, di = r1 + r3, i1 + i3, i3 - i1, r1 - r3
            sections = (
                (ar + cr, ai + ci), (br + dr, bi + di), (ar - cr, ai - ci), (br - dr, bi - di)
            )
            cols = pl.ds(c * 256, 256)
            for q, (sr, si) in enumerate(sections):
                rows = pl.ds(q * FOLD, FOLD)
                tc, ts = twiddle[0, rows, cols], twiddle[1, rows, cols]
                twisted[0, rows, cols] = (sr * tc - si * ts).astype(jnp.bfloat16)
                twisted[1, rows, cols] = (sr * ts + si * tc).astype(jnp.bfloat16)
        for q in range(RADIX):
            rows = pl.ds(q * FOLD, FOLD)
            ac = jnp.dot(twisted[0, rows, :], second[...], preferred_element_type=jnp.float32)
            db = jnp.dot(twisted[1, rows, :], second[...], preferred_element_type=jnp.float32)
            a, c, dd, b = ac[:, :HALF], ac[:, HALF:], db[:, :HALF], db[:, HALF:]
            ad, bc = a * a + dd * dd, b * b + c * c
            both = ad + bc
            cross = 2.0 * (c * dd - a * b)
            lane = lax.broadcasted_iota(jnp.int32, both.shape, 1)
            edge = lane == 0
            both, cross = jnp.where(edge, 0.5 * both, both), jnp.where(edge, 0.5 * (ad - bc), cross)

            @pl.when(d == 0)
            def _():
                total_q[rows, :] = both
                total_r[rows, :] = cross

            @pl.when(d > 0)
            def _():
                total_q[rows, :] += both
                total_r[rows, :] += cross
        return 0

    lax.fori_loop(0, dets, one_detector, 0)

    def largest(i, acc):
        rows = pl.ds(pl.multiple_of(i * 32, 32), 32)
        return jnp.maximum(acc, total_q[rows, :] + jnp.abs(total_r[rows, :]))

    return jnp.max(lax.fori_loop(0, ROWS // 32, largest, jnp.zeros((32, HALF), jnp.float32)))


def body(width, strain_slots, templates, cutoffs, lists, owner, slides):
    n, groups = lax.axis_size("tpl"), lax.axis_size("grp")
    depth = n // 2 // width
    dets, bins = strain_slots.shape[1], strain_slots.shape[3]
    blocks = bins // LANES
    strain = strain_slots[0].reshape(dets, 2, blocks, LANES).transpose(0, 2, 1, 3).reshape(dets, 2 * blocks, LANES)
    count, shard = templates.shape[0], templates.shape[2]
    bank = templates.reshape(count, 2, shard // LANES, LANES).transpose(0, 2, 1, 3)
    bank = bank.reshape(count, 2 * shard // LANES, LANES)
    slots = lists.shape[1]
    first, twiddle, second = constant_tables()
    smem = pl.BlockSpec(memory_space=pltpu.SMEM)
    hbm = pl.BlockSpec(memory_space=pltpu.HBM)
    dma = pltpu.SemaphoreType.DMA
    out = jax.ShapeDtypeStruct((slots,), jnp.float32)
    half, bf16, f32 = blocks, jnp.bfloat16, jnp.float32
    prow = half // (width * depth)
    hrow = bank.shape[1] // groups
    return pl.pallas_call(
        functools.partial(kernel, width),
        out_shape=(out, out),
        in_specs=[smem] * 4 + [hbm] * 5,
        out_specs=(smem, smem),
        scratch_shapes=[
            pltpu.VMEM((dets, half, LANES), bf16),
            pltpu.VMEM((dets, half, LANES), bf16),
            pltpu.VMEM((dets, depth, prow, LANES), bf16),
            pltpu.VMEM((dets, depth, prow, LANES), bf16),
            pltpu.VMEM((2, dets, depth, prow, LANES), bf16),
            pltpu.VMEM((dets, 2 * half, LANES), bf16),
            pltpu.VMEM(bank.shape, bf16),
            pltpu.VMEM((slots, n, hrow, LANES), bf16),
            pltpu.VMEM((slots, n, bank.shape[1], LANES), bf16),
            pltpu.VMEM((TALL, LANES), f32),
            pltpu.VMEM((dets, 2, FOLD, LANES), f32),
            pltpu.VMEM((dets, 2, 8, WIDE), f32),
            pltpu.VMEM((dets, 2, FOLD, WIDE), f32),
            pltpu.VMEM((2, FOLD, WIDE), f32),
            pltpu.VMEM((2, ROWS, COLS), bf16),
            pltpu.VMEM((ROWS, HALF), f32),
            pltpu.VMEM((ROWS, HALF), f32),
            pltpu.VMEM(first.shape, bf16),
            pltpu.VMEM(twiddle.shape, f32),
            pltpu.VMEM(second.shape, bf16),
            dma((5,)),
            dma((dets, width * depth)), dma((dets, width * depth)),
            dma((dets, depth)), dma((dets, depth)),
            dma((2, dets, depth)), dma((2, dets, depth)),
            dma((2, dets, depth)), dma((2, dets, depth)),
            dma((dets, depth)), dma((dets, depth)),
            dma((dets, width * depth)), dma((dets, width * depth)),
            dma((slots, n)), dma((slots, n)),
            dma((slots, max(1, groups - 1), n)), dma((slots, max(1, groups - 1), n)),
        ],
        compiler_params=pltpu.CompilerParams(
            collective_id=0, has_side_effects=True, vmem_limit_bytes=56 * 1024 * 1024
        ),
        name="search",
    )(
        lists.T, owner, cutoffs, slides, strain, bank,
        jnp.asarray(first), jnp.asarray(twiddle), jnp.asarray(second),
    )


def solution(mesh):
    in_specs = (
        P(("grp", "tpl"), None, None, None),
        P(None, None, "tpl"),
        P(),
        P(),
        P("grp"),
        P("grp"),
    )
    out_specs = (P(("grp", "tpl")), P(("grp", "tpl")))
    width = len({d.coords[1] for d in mesh.devices[0].flat})
    return jax.shard_map(
        functools.partial(body, width), mesh=mesh, in_specs=in_specs, out_specs=out_specs, check_vma=False
    )
```

```python
import jax
import jax.numpy as jnp
import numpy as np
from jax import lax
from jax.experimental import pallas as pl
from jax.experimental.pallas import tpu as pltpu
from jax.sharding import PartitionSpec as P

ROWS = 512
COLS = 512
RADIX = 4
FOLD = ROWS // RADIX
WIDE = RADIX * COLS
HALF = COLS // 2
LANES = 128
CHUNKS = WIDE // LANES
TALL = 2 * FOLD * CHUNKS

two_pi = 6.283185307179586
eps_norm = 1e-06

MESH = pl.DeviceIdType.MESH
CUT = 2
CROSS_LAG = 2
PER_STEP = 4


def turn_table(left_ids, right_ids, period):
    product_idx = left_ids[:, None] * right_ids[None, :] % period
    angles = product_idx.astype(np.float32) * np.float32(two_pi / period)
    return np.cos(angles), np.sin(angles)


def constant_tables():
    ids = np.arange(ROWS, dtype=np.int32)
    cos, sin = turn_table(ids[:FOLD], ids, ROWS)
    first = []
    for r in range(RADIX):
        c, s = cos[:, r::RADIX], sin[:, r::RADIX]
        first.append(np.concatenate([np.concatenate([c, -s], 1), np.concatenate([s, c], 1)], 0))
    twiddle = np.stack(turn_table(ids, ids, ROWS * COLS))
    cos, sin = turn_table(ids, ids[: HALF + 1], COLS)
    sin = sin[:, :HALF].copy()
    sin[:, 0] = cos[:, HALF]
    second = np.concatenate([cos[:, :HALF], sin], 1)
    return np.stack(first).astype(jnp.bfloat16), twiddle, second.astype(jnp.bfloat16)


def kernel(
    lists, owner, cutoffs, slides, strain, bank_hbm, first_hbm, twiddle_hbm, second_hbm,
    results,
    cand, other, heap, full, bank, picked, arrived, flat, row_phase, col_phase,
    turned, masked, twisted, total_q, total_r, squares, first, twiddle, second,
    local_sem, near_sem, core_send, core_recv, rs_send, rs_recv, ag_send, ag_recv,
    part_send, part_recv, swap_send, swap_recv, cross_send, cross_recv,
):
    n, groups = lax.axis_size("tpl"), lax.axis_size("grp")
    me, group = lax.axis_index("tpl"), lax.axis_index("grp")
    bits = n.bit_length() - 2
    core, chip = me % 2, me // 2
    dets = strain.shape[0] // (2 * CUT)
    units = dets * CUT
    half = strain.shape[1]
    slots = lists.shape[0]
    shard = bank.shape[1]
    hrow = shard // groups

    own_id = owner[0]
    own_chip = own_id // 2
    i_own = own_id == me

    bit = [chip // (1 << k) % 2 for k in range(bits)]
    base = [0]
    for k in range(bits):
        base.append(base[k] + bit[k] * (half >> (k + 1)))

    def flip(mask):
        return me + sum((mask & b) - 2 * (mask & b) * (me // b % 2) for b in (1 << i for i in range(n.bit_length() - 1)) if mask & b)

    partner = flip(1)
    peers = [flip(2 << k) for k in range(bits)]

    def remote(src, dst, send, recv, **where):
        return pltpu.make_async_remote_copy(
            src_ref=src, dst_ref=dst, send_sem=send, recv_sem=recv, device_id=where, device_id_type=MESH
        )

    def rows(start, size):
        return pl.ds(pl.multiple_of(start, 16), size)

    def core_copy(u):
        return remote(strain.at[2 * u + 1 - core], other.at[u], core_send.at[u], core_recv.at[u], tpl=partner)

    def away(k):
        size = half >> (k + 1)
        return rows(base[k] + (1 - bit[k]) * size, size)

    def kept(k):
        return rows(base[k], half >> k)

    def pile(k):
        return pl.ds(half - (half >> k), half >> (k + 1))

    def rs_copy(u, k):
        return remote(
            cand.at[u, away(k)], heap.at[u, pile(k)], rs_send.at[k, u], rs_recv.at[k, u], tpl=peers[k]
        )

    def ag_copy(u, k):
        at = full.at[2 * u + core, kept(k + 1)]
        return remote(at, at, ag_send.at[k, u], ag_recv.at[k, u], tpl=peers[k])

    def ag_arrival(u, k):
        at = full.at[2 * u + core, away(k)]
        return remote(at, at, ag_send.at[k, u], ag_recv.at[k, u], tpl=peers[k])

    def part_copy(u, cc, which):
        at = full.at[2 * u + cc, kept(1) if which == 0 else away(0)]
        return remote(at, at, part_send.at[which, u], part_recv.at[which, u], tpl=partner)

    def swap_peer(i):
        to = 0
        for b in (1 << e for e in range(n.bit_length() - 1)):
            to = to + (i // b % 2 + me // b % 2) % 2 * b
        return to

    def swap_copy(slot, i):
        to = swap_peer(i)
        return remote(
            picked.at[slot, to], arrived.at[slot, me, rows(group * hrow, hrow)],
            swap_send.at[slot, i], swap_recv.at[slot, i], tpl=to,
        )

    def swap_arrival(slot, i):
        source = swap_peer(i)
        return remote(
            picked.at[slot, me], arrived.at[slot, source, rows(group * hrow, hrow)],
            swap_send.at[slot, i], swap_recv.at[slot, i], tpl=source,
        )

    def cross_copy(slot, i, g):
        at = arrived.at[slot, swap_peer(i), rows(group * hrow, hrow)]
        return remote(
            at, at, cross_send.at[slot, g - 1, i], cross_recv.at[slot, g - 1, i], grp=(group + g) % groups
        )

    def cross_arrival(slot, i, g):
        source = (group - g + groups) % groups
        at = arrived.at[slot, swap_peer(i), rows(source * hrow, hrow)]
        return remote(at, at, cross_send.at[slot, g - 1, i], cross_recv.at[slot, g - 1, i], grp=source)

    tables = [
        pltpu.make_async_copy(first_hbm, first, local_sem.at[2]),
        pltpu.make_async_copy(twiddle_hbm, twiddle, local_sem.at[3]),
        pltpu.make_async_copy(second_hbm, second, local_sem.at[4]),
    ]
    mine_copies = [
        pltpu.make_async_copy(strain.at[2 * u + core], cand.at[u], local_sem.at[5 + u]) for u in range(units)
    ]
    bank_copy = pltpu.make_async_copy(bank_hbm, bank, local_sem.at[0])
    for copy in mine_copies:
        copy.start()
    bank_copy.start()

    barrier = pltpu.get_barrier_semaphore()
    for peer in [partner] + peers:
        pl.semaphore_signal(barrier, inc=1, device_id={"tpl": peer}, device_id_type=MESH)
    for g in range(1, groups):
        pl.semaphore_signal(barrier, inc=1, device_id={"grp": (group + g) % groups}, device_id_type=MESH)
    make_phases(slides, row_phase, col_phase)
    pl.semaphore_wait(barrier, bits + groups)

    for u in range(units):
        core_copy(u).start()

    def greet(k):
        pl.semaphore_signal(near_sem.at[k], inc=1, device_id={"tpl": ([partner] + peers)[k]}, device_id_type=MESH)

    def choice(u, where):
        cand[u, where] = jnp.where(i_own, cand[u, where], other[u, where])

    greet(0)
    for u in range(units):
        mine_copies[u].wait()
        core_copy(u).wait_recv()
        choice(u, away(0))
        rs_copy(u, 0).start()
        choice(u, kept(1))
        if u < bits:
            pl.semaphore_wait(near_sem.at[u], 1)
            if u + 1 < bits:
                greet(u + 1)
    for u in range(units, bits):
        pl.semaphore_wait(near_sem.at[u], 1)
        if u + 1 < bits:
            greet(u + 1)
    for copy in tables:
        copy.start()
    bank_copy.wait()
    for slot in range(slots):
        arrived[slot, me] = bank[lists[slot, me]]

    def merge(u, k, where, start, size):
        agree = own_chip // (1 << k) == chip // (1 << k)
        offset = half - (half >> k) + start - base[k + 1]
        return jnp.where(agree, cand[u, where], heap[u, rows(offset, size)])

    def stage(u, e):
        if e < bits:
            k = e
            rs_copy(u, k).wait_recv()
            if k + 1 < bits:
                size = half >> (k + 2)
                start = base[k + 1] + (1 - bit[k + 1]) * size
                cand[u, away(k + 1)] = merge(u, k, away(k + 1), start, size)
                rs_copy(u, k + 1).start()
                cand[u, kept(k + 2)] = merge(u, k, kept(k + 2), base[k + 2], size)
            else:
                full[2 * u + core, kept(bits)] = merge(u, k, kept(bits), base[bits], half >> bits)
                ag_copy(u, bits - 1).start()
        else:
            k = 2 * bits - 1 - e
            ag_arrival(u, k).wait_recv()
            if k > 0:
                ag_copy(u, k - 1).start()
            if k < 2:
                part_copy(u, core, 1 - k).start()

    messages = slots * (n - 1)
    per_step = max(PER_STEP, -(-messages // (units + 2 * bits - CROSS_LAG)))
    landed = [((n - 1) * (slot + 1) - 1) // per_step + CROSS_LAG for slot in range(slots)]
    turn_at = [u + 2 * bits for u in range(units)]
    clock = 0
    mask_at, filter_at = [], []
    for slot in range(slots):
        mask_at.append(landed[slot] + 1)
    pairs = sorted(
        (max(turn_at[CUT * (d + 1) - 1], mask_at[slot]), d, slot) for d in range(dets) for slot in range(slots)
    )
    for ready, d, slot in pairs:
        clock = max(clock + 1, ready)
        filter_at.append((clock, slot, d))
    steps = max(clock, units + 2 * bits, per_step) + 1

    def swap_start(q):
        slot, i = q // (n - 1), n - 1 - q % (n - 1)
        to = swap_peer(i)
        picked[slot, to] = bank[lists[slot, to], rows(group * hrow, hrow)]
        swap_copy(slot, i).start()

    def cross_start(q):
        slot, i = q // (n - 1), n - 1 - q % (n - 1)
        swap_arrival(slot, i).wait_recv()
        for g in range(1, groups):
            cross_copy(slot, i, g).start()

    def choose(t, pairs):
        value, hit = 0, False
        for at, v in pairs:
            value, hit = jnp.where(t == at, v, value), (t == at) | hit
        return value, hit

    def step_body(t, _):
        for e in range(2 * bits):
            u = t - e

            @pl.when((u >= 0) & (u < units))
            def _():
                stage(u, e)

        for e in range(per_step):
            q = t * per_step + e

            @pl.when(q < messages)
            def _():
                swap_start(q)

            p = (t - CROSS_LAG) * per_step + e

            @pl.when((p >= 0) & (p < messages))
            def _():
                cross_start(p)

        u, now = choose(t, list(zip(turn_at, range(units))))

        @pl.when(now)
        def _():
            for which in range(2):
                part_arrival(u, which).wait_recv()
            turn_unit(full.at[pl.ds(2 * u, 2)], flat, row_phase, col_phase, turned, u // CUT, u % CUT)

        slot, now = choose(t, list(zip(mask_at, range(slots))))

        @pl.when(now)
        def _():
            def join(i, _):
                for g in range(1, groups):
                    cross_arrival(slot, i, g).wait_recv()
                return 0

            lax.fori_loop(1, n, join, 0)
            cutoff = cutoffs[lists[slot, me]]
            squares[slot] = mask_template(cutoff, arrived.at[slot], flat, masked.at[slot])

        pair, now = choose(t, [(at, slot * dets + d) for at, slot, d in filter_at])

        @pl.when(now)
        def _():
            slot, d = pair // dets, pair % dets
            filter_detector(
                d, turned.at[d], masked.at[slot], first, twiddle, second, twisted,
                total_q.at[slot], total_r.at[slot],
            )

        return 0

    def part_arrival(u, which):
        at = full.at[2 * u + 1 - core, kept(1) if which == 0 else away(0)]
        return remote(at, at, part_send.at[which, u], part_recv.at[which, u], tpl=partner)

    for copy in tables:
        copy.wait()
    lax.fori_loop(0, steps, step_body, 0)

    def drain(u, _):
        core_copy(u).wait_send()
        for k in range(bits):
            rs_copy(u, k).wait_send()
            ag_copy(u, k).wait_send()
        for which in range(2):
            part_copy(u, core, which).wait_send()
        return 0

    lax.fori_loop(0, units, drain, 0)

    def finish_swap(i, _):
        for slot in range(slots):
            swap_copy(slot, i).wait_send()
            for g in range(1, groups):
                cross_copy(slot, i, g).wait_send()
        return 0

    lax.fori_loop(1, n, finish_swap, 0)
    for slot in range(slots):
        sigmasq = jnp.sum(squares[slot])
        results[slot] = largest(total_q.at[slot], total_r.at[slot]) / (2.0 * (sigmasq + eps_norm))
        results[slots + slot] = sigmasq / (ROWS * COLS)


def make_phases(slides, row_phase, col_phase):
    total = ROWS * COLS
    for d in range(row_phase.shape[0]):
        slide = slides[d]
        row = lax.broadcasted_iota(jnp.int32, (FOLD, LANES), 0) * slide % FOLD
        row = row.astype(jnp.float32) * (two_pi / FOLD)
        row_phase[d, 0] = jnp.cos(row)
        row_phase[d, 1] = jnp.sin(row)
        col = lax.broadcasted_iota(jnp.int32, (8, WIDE), 1) * slide % total
        col = col.astype(jnp.float32) * (two_pi / total)
        col_phase[d, 0] = jnp.cos(col)
        col_phase[d, 1] = jnp.sin(col)


def tile(flat, i, c, part):
    return flat[pl.ds((i * 8 * CHUNKS + c) * 2 + part, 8, stride=2 * CHUNKS), :]


def turn_unit(source, flat, row_phase, col_phase, turned, d, q):
    half, size = source.shape[1], 256
    high = FOLD // CUT

    def widen(i, _):
        for h in range(2):
            at = pl.ds(pl.multiple_of(i * size, size), size)
            flat[pl.ds(pl.multiple_of(h * half + i * size, size), size), :] = source[h, at, :].astype(jnp.float32)
        return 0

    lax.fori_loop(0, half // size, widen, 0)

    def body(i, _):
        at = pl.ds(pl.multiple_of(q * high + i * 8, 8), 8)
        rr, ri = row_phase[d, 0, at, :], row_phase[d, 1, at, :]
        for c in range(CHUNKS):
            cols = pl.ds(c * LANES, LANES)
            cr, ci = col_phase[d, 0, :, cols], col_phase[d, 1, :, cols]
            pr, pi = rr * cr - ri * ci, rr * ci + ri * cr
            xr, xi = tile(flat, i, c, 0), tile(flat, i, c, 1)
            turned[d, 0, at, cols] = xr * pr - xi * pi
            turned[d, 1, at, cols] = xr * pi + xi * pr
        return 0

    lax.fori_loop(0, high // 8, body, 0)


def mask_template(cutoff, source, flat, masked):
    shards, shard = source.shape[0], source.shape[1]

    def body(i, _):
        flat[pl.ds(pl.multiple_of(i * shard, shard), shard), :] = source[i].astype(jnp.float32)
        return 0

    lax.fori_loop(0, shards, body, 0)

    def mask(i, acc):
        at = pl.ds(pl.multiple_of(i * 8, 8), 8)
        base = (lax.broadcasted_iota(jnp.int32, (8, LANES), 0) + i * 8) * WIDE + lax.broadcasted_iota(
            jnp.int32, (8, LANES), 1
        )
        for c in range(CHUNKS):
            cols = pl.ds(c * LANES, LANES)
            inside = base < cutoff - c * LANES
            wr = jnp.where(inside, tile(flat, i, c, 0), 0.0)
            wi = jnp.where(inside, tile(flat, i, c, 1), 0.0)
            masked[0, at, cols] = wr
            masked[1, at, cols] = wi
            acc = acc + (wr * wr + wi * wi)
        return acc

    return lax.fori_loop(0, FOLD // 8, mask, jnp.zeros((8, LANES), jnp.float32))


def filter_detector(d, turned, masked, first, twiddle, second, twisted, total_q, total_r):
    for c in range(COLS // 256):
        parts = []
        for r in range(RADIX):
            cols = pl.ds(r * COLS + c * 256, 256)
            xr, xi = turned[0, :, cols], turned[1, :, cols]
            wr, wi = masked[0, :, cols], masked[1, :, cols]
            product = jnp.concatenate([xr * wr + xi * wi, xi * wr - xr * wi], 0)
            out = jnp.dot(first[r], product.astype(jnp.bfloat16), preferred_element_type=jnp.float32)
            parts.append((out[:FOLD], out[FOLD:]))
        (r0, i0), (r1, i1), (r2, i2), (r3, i3) = parts
        ar, ai, br, bi = r0 + r2, i0 + i2, r0 - r2, i0 - i2
        cr, ci, dr, di = r1 + r3, i1 + i3, i3 - i1, r1 - r3
        sections = (
            (ar + cr, ai + ci), (br + dr, bi + di), (ar - cr, ai - ci), (br - dr, bi - di)
        )
        cols = pl.ds(c * 256, 256)
        for q, (sr, si) in enumerate(sections):
            rows = pl.ds(q * FOLD, FOLD)
            tc, ts = twiddle[0, rows, cols], twiddle[1, rows, cols]
            twisted[0, rows, cols] = (sr * tc - si * ts).astype(jnp.bfloat16)
            twisted[1, rows, cols] = (sr * ts + si * tc).astype(jnp.bfloat16)
    for q in range(RADIX):
        rows = pl.ds(q * FOLD, FOLD)
        ac = jnp.dot(twisted[0, rows, :], second[...], preferred_element_type=jnp.float32)
        db = jnp.dot(twisted[1, rows, :], second[...], preferred_element_type=jnp.float32)
        a, c, dd, b = ac[:, :HALF], ac[:, HALF:], db[:, :HALF], db[:, HALF:]
        ad, bc = a * a + dd * dd, b * b + c * c
        both = ad + bc
        cross = 2.0 * (c * dd - a * b)
        lane = lax.broadcasted_iota(jnp.int32, both.shape, 1)
        edge = lane == 0
        both, cross = jnp.where(edge, 0.5 * both, both), jnp.where(edge, 0.5 * (ad - bc), cross)

        @pl.when(d == 0)
        def _():
            total_q[rows, :] = both
            total_r[rows, :] = cross

        @pl.when(d > 0)
        def _():
            total_q[rows, :] += both
            total_r[rows, :] += cross

def largest(total_q, total_r):
    def body(i, acc):
        rows = pl.ds(pl.multiple_of(i * 32, 32), 32)
        return jnp.maximum(acc, total_q[rows, :] + jnp.abs(total_r[rows, :]))

    return jnp.max(lax.fori_loop(0, ROWS // 32, body, jnp.zeros((32, HALF), jnp.float32)))


def body(strain_slots, templates, cutoffs, lists, owner, slides):
    n, groups = lax.axis_size("tpl"), lax.axis_size("grp")
    bits = n.bit_length() - 2
    dets, bins = strain_slots.shape[1], strain_slots.shape[3]
    units, half = dets * CUT, bins // LANES // CUT
    strain = strain_slots[0].reshape(dets, 2, bins // LANES, LANES).transpose(0, 2, 1, 3)
    strain = strain.reshape(2 * units, half, LANES)
    count, shard = templates.shape[0], templates.shape[2]
    bank = templates.reshape(count, 2, shard // LANES, LANES).transpose(0, 2, 1, 3)
    bank = bank.reshape(count, 2 * shard // LANES, LANES)
    slots = lists.shape[1]
    first, twiddle, second = constant_tables()
    smem = pl.BlockSpec(memory_space=pltpu.SMEM)
    hbm = pl.BlockSpec(memory_space=pltpu.HBM)
    dma, bf16, f32 = pltpu.SemaphoreType.DMA, jnp.bfloat16, jnp.float32
    hrow = bank.shape[1] // groups
    results = pl.pallas_call(
        kernel,
        out_shape=jax.ShapeDtypeStruct((2 * slots,), f32),
        in_specs=[smem] * 4 + [hbm] * 5,
        out_specs=smem,
        scratch_shapes=[
            pltpu.VMEM((units, half, LANES), bf16),
            pltpu.VMEM((units, half, LANES), bf16),
            pltpu.VMEM((units, half, LANES), bf16),
            pltpu.VMEM((2 * units, half, LANES), bf16),
            pltpu.VMEM(bank.shape, bf16),
            pltpu.VMEM((slots, n, hrow, LANES), bf16),
            pltpu.VMEM((slots, n, bank.shape[1], LANES), bf16),
            pltpu.VMEM((TALL, LANES), f32),
            pltpu.VMEM((dets, 2, FOLD, LANES), f32),
            pltpu.VMEM((dets, 2, 8, WIDE), f32),
            pltpu.VMEM((dets, 2, FOLD, WIDE), f32),
            pltpu.VMEM((slots, 2, FOLD, WIDE), f32),
            pltpu.VMEM((2, ROWS, COLS), bf16),
            pltpu.VMEM((slots, ROWS, HALF), f32),
            pltpu.VMEM((slots, ROWS, HALF), f32),
            pltpu.VMEM((slots, 8, LANES), f32),
            pltpu.VMEM(first.shape, bf16),
            pltpu.VMEM(twiddle.shape, f32),
            pltpu.VMEM(second.shape, bf16),
            dma((5 + units,)),
            pltpu.SemaphoreType.REGULAR((bits,)),
            dma((units,)), dma((units,)),
            dma((bits, units)), dma((bits, units)),
            dma((bits, units)), dma((bits, units)),
            dma((2, units)), dma((2, units)),
            dma((slots, n)), dma((slots, n)),
            dma((slots, max(1, groups - 1), n)), dma((slots, max(1, groups - 1), n)),
        ],
        compiler_params=pltpu.CompilerParams(
            collective_id=0, has_side_effects=True, vmem_limit_bytes=56 * 1024 * 1024
        ),
        name="search",
    )(
        lists.T, owner, cutoffs, slides, strain, bank,
        jnp.asarray(first), jnp.asarray(twiddle), jnp.asarray(second),
    )
    return results[:slots], results[slots:]


def solution(mesh):
    in_specs = (
        P(("grp", "tpl"), None, None, None),
        P(None, None, "tpl"),
        P(),
        P(),
        P("grp"),
        P("grp"),
    )
    out_specs = (P(("grp", "tpl")), P(("grp", "tpl")))
    return jax.shard_map(body, mesh=mesh, in_specs=in_specs, out_specs=out_specs, check_vma=False)
```

```python
import jax
import jax.numpy as jnp
import numpy as np
from jax import lax
from jax.experimental import pallas as pl
from jax.experimental.pallas import tpu as pltpu
from jax.sharding import PartitionSpec as P

ROWS = 512
COLS = 512
RADIX = 4
FOLD = ROWS // RADIX
WIDE = RADIX * COLS
HALF = COLS // 2
LANES = 128
CHUNKS = WIDE // LANES
TALL = 2 * FOLD * CHUNKS

two_pi = 6.283185307179586
eps_norm = 1e-06

MESH = pl.DeviceIdType.MESH
CUT = 2
EARLY = 8
SWAP_STEP = 4
CROSS_STEP = 5
CROSS_FROM = 1


def turn_table(left_ids, right_ids, period):
    product_idx = left_ids[:, None] * right_ids[None, :] % period
    angles = product_idx.astype(np.float32) * np.float32(two_pi / period)
    return np.cos(angles), np.sin(angles)


def constant_tables():
    ids = np.arange(ROWS, dtype=np.int32)
    cos, sin = turn_table(ids[:FOLD], ids, ROWS)
    first = []
    for r in range(RADIX):
        c, s = cos[:, r::RADIX], sin[:, r::RADIX]
        first.append(np.concatenate([np.concatenate([c, -s], 1), np.concatenate([s, c], 1)], 0))
    twiddle = np.stack(turn_table(ids, ids, ROWS * COLS))
    cos, sin = turn_table(ids, ids[: HALF + 1], COLS)
    sin = sin[:, :HALF].copy()
    sin[:, 0] = cos[:, HALF]
    second = np.concatenate([cos[:, :HALF], sin], 1)
    return np.stack(first).astype(jnp.bfloat16), twiddle, second.astype(jnp.bfloat16)


def kernel(
    lists, owner, cutoffs, slides, strain, bank_hbm, first_hbm, twiddle_hbm, second_hbm,
    results,
    cand, other, heap, full, bank, picked, arrived, flat, row_phase, col_phase,
    turned, masked, twisted, sections, total_q, total_r, squares, first, twiddle, second,
    local_sem, near_sem, core_send, core_recv, rs_send, rs_recv, ag_send, ag_recv,
    part_send, part_recv, swap_send, swap_recv, cross_send, cross_recv,
):
    n, groups = lax.axis_size("tpl"), lax.axis_size("grp")
    me, group = lax.axis_index("tpl"), lax.axis_index("grp")
    bits = n.bit_length() - 2
    core, chip = me % 2, me // 2
    dets = strain.shape[0] // (2 * CUT)
    units = dets * CUT
    half = strain.shape[1]
    slots = lists.shape[0]
    shard = bank.shape[1]
    hrow = shard // groups

    own_id = owner[0]
    own_chip = own_id // 2
    i_own = own_id == me

    bit = [chip // (1 << k) % 2 for k in range(bits)]
    base = [0]
    for k in range(bits):
        base.append(base[k] + bit[k] * (half >> (k + 1)))

    turns = [(1 << k) * (1 - 2 * (me // (1 << k) % 2)) for k in range(bits + 1)]

    def flip(mask):
        return me + sum(turns[k] for k in range(bits + 1) if mask >> k & 1)

    partner = flip(1)
    peers = [flip(2 << k) for k in range(bits)]

    def remote(src, dst, send, recv, **where):
        return pltpu.make_async_remote_copy(
            src_ref=src, dst_ref=dst, send_sem=send, recv_sem=recv, device_id=where, device_id_type=MESH
        )

    def rows(start, size):
        return pl.ds(pl.multiple_of(start, 16), size)

    def core_copy(u):
        return remote(strain.at[2 * u + 1 - core], other.at[u], core_send, core_recv.at[u], tpl=partner)

    def away(k):
        size = half >> (k + 1)
        return rows(base[k] + (1 - bit[k]) * size, size)

    def kept(k):
        return rows(base[k], half >> k)

    def pile(k):
        return pl.ds(half - (half >> k), half >> (k + 1))

    def rs_copy(u, k):
        return remote(
            cand.at[u, away(k)], heap.at[u, pile(k)], rs_send, rs_recv.at[k, u], tpl=peers[k]
        )

    def ag_copy(u, k):
        at = full.at[2 * u + core, kept(k + 1)]
        return remote(at, at, ag_send, ag_recv.at[k, u], tpl=peers[k])

    def ag_arrival(u, k):
        at = full.at[2 * u + core, away(k)]
        return remote(at, at, ag_send, ag_recv.at[k, u], tpl=peers[k])

    def part_copy(u, cc, which):
        at = full.at[2 * u + cc, kept(1) if which == 0 else away(0)]
        return remote(at, at, part_send, part_recv.at[which, u], tpl=partner)

    def swap_copy(slot, i):
        to = flip(i)
        return remote(
            picked.at[slot, to], arrived.at[slot, me, rows(group * hrow, hrow)],
            swap_send, swap_recv.at[slot, i], tpl=to,
        )

    def swap_arrival(slot, i):
        source = flip(i)
        return remote(
            picked.at[slot, me], arrived.at[slot, source, rows(group * hrow, hrow)],
            swap_send, swap_recv.at[slot, i], tpl=source,
        )

    def cross_copy(slot, i, g):
        at = arrived.at[slot, flip(i), rows(group * hrow, hrow)]
        return remote(
            at, at, cross_send.at[g - 1], cross_recv.at[slot, g - 1], grp=(group + g) % groups
        )

    def cross_arrivals(slot, g):
        at = picked.at[slot, pl.ds(0, n - 1)]
        return remote(
            at, at, cross_send.at[g - 1], cross_recv.at[slot, g - 1], grp=(group + g) % groups
        )

    tables = [
        pltpu.make_async_copy(first_hbm, first, local_sem.at[2]),
        pltpu.make_async_copy(twiddle_hbm, twiddle, local_sem.at[3]),
        pltpu.make_async_copy(second_hbm, second, local_sem.at[4]),
    ]
    mine_copies = [
        pltpu.make_async_copy(strain.at[2 * u + core], cand.at[u], local_sem.at[5 + u]) for u in range(units)
    ]
    bank_copy = pltpu.make_async_copy(bank_hbm, bank, local_sem.at[0])
    for copy in mine_copies:
        copy.start()
    bank_copy.start()

    barrier = pltpu.get_barrier_semaphore()
    for peer in [partner] + peers:
        pl.semaphore_signal(barrier, inc=1, device_id={"tpl": peer}, device_id_type=MESH)
    for g in range(1, groups):
        pl.semaphore_signal(barrier, inc=1, device_id={"grp": (group + g) % groups}, device_id_type=MESH)
    pl.semaphore_wait(barrier, bits + groups)

    for u in range(units):
        core_copy(u).start()

    def greet(k):
        pl.semaphore_signal(near_sem.at[k], inc=1, device_id={"tpl": ([partner] + peers)[k]}, device_id_type=MESH)

    def choice(u, where):
        cand[u, where] = jnp.where(i_own, cand[u, where], other[u, where])

    greet(0)
    for u in range(units):
        mine_copies[u].wait()
        core_copy(u).wait_recv()
        choice(u, away(0))
        rs_copy(u, 0).start()
        choice(u, kept(1))
        if u < bits:
            pl.semaphore_wait(near_sem.at[u], 1)
            if u + 1 < bits:
                greet(u + 1)
    for u in range(units, bits):
        pl.semaphore_wait(near_sem.at[u], 1)
        if u + 1 < bits:
            greet(u + 1)
    bank_copy.wait()
    apart = sorted(range(2, n), key=lambda i: (i & 2, -i))
    alone = sum(1 for i in apart if not i & 2)
    queue = [(slot, 1) for slot in range(slots)]
    queue += [(slot, i) for slot in range(slots) for i in apart[:alone]]
    queue += [(slot, i) for slot in range(slots) for i in apart[alone:]]
    early = max(0, min(EARLY, len(queue)))

    def swap_start(q):
        slot, i = queue[q]
        to = flip(i)
        picked[slot, to] = bank[lists[slot, to], rows(group * hrow, hrow)]
        swap_copy(slot, i).start()

    def cross_start(q):
        slot, i = queue[q]
        swap_arrival(slot, i).wait_recv()
        for g in range(1, groups):
            cross_copy(slot, i, g).start()

    for q in range(early):
        swap_start(q)
    for copy in tables:
        copy.start()
    make_phases(slides, row_phase, col_phase)
    for slot in range(slots):
        arrived[slot, me] = bank[lists[slot, me]]
    total_q[...] = jnp.zeros_like(total_q)
    total_r[...] = jnp.zeros_like(total_r)

    def merge(u, k, where, start, size):
        agree = own_chip // (1 << k) == chip // (1 << k)
        offset = half - (half >> k) + start - base[k + 1]
        return jnp.where(agree, cand[u, where], heap[u, rows(offset, size)])

    def stage(u, e):
        if e < bits:
            k = e
            rs_copy(u, k).wait_recv()
            if k + 1 < bits:
                size = half >> (k + 2)
                start = base[k + 1] + (1 - bit[k + 1]) * size
                cand[u, away(k + 1)] = merge(u, k, away(k + 1), start, size)
                rs_copy(u, k + 1).start()
                cand[u, kept(k + 2)] = merge(u, k, kept(k + 2), base[k + 2], size)
            else:
                full[2 * u + core, kept(bits)] = merge(u, k, kept(bits), base[bits], half >> bits)
                ag_copy(u, bits - 1).start()
        else:
            k = 2 * bits - 1 - e
            ag_arrival(u, k).wait_recv()
            if k > 0:
                ag_copy(u, k - 1).start()
            if k < 2:
                part_copy(u, core, 1 - k).start()

    talk = units + 2 * bits - 1
    swap_step = max(SWAP_STEP, -(-(len(queue) - early) // (talk - 3)))
    cross_step = max(CROSS_STEP, -(-len(queue) // (talk - CROSS_FROM)))
    swap_slots = [range(early + t * swap_step, min(len(queue), early + (t + 1) * swap_step)) for t in range(talk)]
    ends = [min(len(queue), (t - CROSS_FROM + 1) * cross_step, early + max(0, t - 1) * swap_step) for t in range(talk)]
    ends = [max(0, end) if t >= CROSS_FROM else 0 for t, end in enumerate(ends)] + [len(queue)]
    cross_slots = [range(ends[t - 1] if t else 0, ends[t]) for t in range(talk + 1)]
    swap_slots.append(())
    talk += 1
    landed = [
        max(t for t in range(talk) if any(queue[q][0] == slot for q in cross_slots[t])) for slot in range(slots)
    ]
    turn_at = [u + 2 * bits for u in range(units)]
    mask_at = [at + 1 for at in landed]
    pairs = sorted(
        (max(turn_at[CUT * (d + 1) - 1], mask_at[slot]), d, slot) for d in range(dets) for slot in range(slots)
    )
    filter_at = [ready for ready, _, _ in pairs]
    steps = max(filter_at[-1], units + 2 * bits, landed[-1]) + 1

    def choose(t, pairs):
        value, hit = 0, False
        for at, v in pairs:
            value, hit = jnp.where(t == at, v, value), (t == at) | hit
        return value, hit

    def step_body(t, _):
        for at in range(talk):
            @pl.when(t == at)
            def _():
                for e in range(2 * bits):
                    if 0 <= at - e < units:
                        stage(at - e, e)
                for q in cross_slots[at]:
                    cross_start(q)
                for q in swap_slots[at]:
                    swap_start(q)

        u, now = choose(t, list(zip(turn_at, range(units))))

        @pl.when(now)
        def _():
            for which in range(2):
                part_arrival(u, which).wait_recv()
            turn_unit(full.at[pl.ds(2 * u, 2)], flat, row_phase, col_phase, turned, u // CUT, u % CUT)

        slot, now = choose(t, list(zip(mask_at, range(slots))))

        @pl.when(now)
        def _():
            for g in range(1, groups):
                cross_arrivals(slot, g).wait_recv()
            cutoff = cutoffs[lists[slot, me]]
            squares[slot] = mask_template(cutoff, arrived.at[slot], flat, masked.at[slot])

        def one_filter(f, _):
            slot = choose(f, [(k, pair[2]) for k, pair in enumerate(pairs)])[0]
            d = choose(f, [(k, pair[1]) for k, pair in enumerate(pairs)])[0]
            filter_detector(
                turned.at[d], masked.at[slot], first, twiddle, second, twisted, sections,
                total_q.at[slot], total_r.at[slot],
            )
            return 0

        begin = sum((t > at).astype(jnp.int32) for at in filter_at)
        end = sum((t >= at).astype(jnp.int32) for at in filter_at)
        lax.fori_loop(begin, end, one_filter, 0)
        return 0

    def part_arrival(u, which):
        at = full.at[2 * u + 1 - core, kept(1) if which == 0 else away(0)]
        return remote(at, at, part_send, part_recv.at[which, u], tpl=partner)

    for copy in tables:
        copy.wait()
    lax.fori_loop(0, steps, step_body, 0)

    def sent(at, semaphore):
        remote(at, at, semaphore, core_recv.at[0], tpl=partner).wait_send()

    walk = heap.at[:, pl.ds(0, half - (half >> bits))]
    for at, semaphore in (
        (other, core_send), (walk, rs_send), (walk, ag_send), (other, part_send),
        (picked.at[:, pl.ds(0, n - 1)], swap_send),
    ):
        sent(at, semaphore)
    for g in range(1, groups):
        sent(picked.at[:, pl.ds(0, n - 1)], cross_send.at[g - 1])
    for slot in range(slots):
        sigmasq = jnp.sum(squares[slot])
        results[slot] = largest(total_q.at[slot], total_r.at[slot]) / (2.0 * (sigmasq + eps_norm))
        results[slots + slot] = sigmasq / (ROWS * COLS)


def make_phases(slides, row_phase, col_phase):
    total = ROWS * COLS

    def body(d, _):
        slide = slides[d]
        row = lax.broadcasted_iota(jnp.int32, (FOLD, LANES), 0) * slide % FOLD
        row = row.astype(jnp.float32) * (two_pi / FOLD)
        row_phase[d, 0] = jnp.cos(row)
        row_phase[d, 1] = jnp.sin(row)
        col = lax.broadcasted_iota(jnp.int32, (8, WIDE), 1) * slide % total
        col = col.astype(jnp.float32) * (two_pi / total)
        col_phase[d, 0] = jnp.cos(col)
        col_phase[d, 1] = jnp.sin(col)
        return 0

    lax.fori_loop(0, row_phase.shape[0], body, 0)


def tile(flat, i, c, part):
    return flat[pl.ds((i * 8 * CHUNKS + c) * 2 + part, 8, stride=2 * CHUNKS), :]


def turn_unit(source, flat, row_phase, col_phase, turned, d, q):
    half, size = source.shape[1], 256
    high = FOLD // CUT

    def widen(i, _):
        for h in range(2):
            at = pl.ds(pl.multiple_of(i * size, size), size)
            flat[pl.ds(pl.multiple_of(h * half + i * size, size), size), :] = source[h, at, :].astype(jnp.float32)
        return 0

    lax.fori_loop(0, half // size, widen, 0)

    def body(i, _):
        at = pl.ds(pl.multiple_of(q * high + i * 8, 8), 8)
        rr, ri = row_phase[d, 0, at, :], row_phase[d, 1, at, :]
        for c in range(CHUNKS):
            cols = pl.ds(c * LANES, LANES)
            cr, ci = col_phase[d, 0, :, cols], col_phase[d, 1, :, cols]
            pr, pi = rr * cr - ri * ci, rr * ci + ri * cr
            xr, xi = tile(flat, i, c, 0), tile(flat, i, c, 1)
            turned[d, 0, at, cols] = xr * pr - xi * pi
            turned[d, 1, at, cols] = xr * pi + xi * pr
        return 0

    lax.fori_loop(0, high // 8, body, 0)


def mask_template(cutoff, source, flat, masked):
    shards, shard = source.shape[0], source.shape[1]

    def body(i, _):
        flat[pl.ds(pl.multiple_of(i * shard, shard), shard), :] = source[i].astype(jnp.float32)
        return 0

    lax.fori_loop(0, shards, body, 0)

    def mask(i, acc):
        at = pl.ds(pl.multiple_of(i * 8, 8), 8)
        base = (lax.broadcasted_iota(jnp.int32, (8, LANES), 0) + i * 8) * WIDE + lax.broadcasted_iota(
            jnp.int32, (8, LANES), 1
        )
        for c in range(CHUNKS):
            cols = pl.ds(c * LANES, LANES)
            inside = base < cutoff - c * LANES
            wr = jnp.where(inside, tile(flat, i, c, 0), 0.0)
            wi = jnp.where(inside, tile(flat, i, c, 1), 0.0)
            masked[0, at, cols] = wr
            masked[1, at, cols] = wi
            acc = acc + (wr * wr + wi * wi)
        return acc

    return lax.fori_loop(0, FOLD // 8, mask, jnp.zeros((8, LANES), jnp.float32))


def filter_detector(turned, masked, first, twiddle, second, twisted, sections, total_q, total_r):
    for c in range(COLS // 256):
        for r in range(RADIX):
            cols = pl.ds(r * COLS + c * 256, 256)
            xr, xi = turned[0, :, cols], turned[1, :, cols]
            wr, wi = masked[0, :, cols], masked[1, :, cols]
            product = jnp.concatenate([xr * wr + xi * wi, xi * wr - xr * wi], 0)
            sections[c, r] = jnp.dot(first[r], product.astype(jnp.bfloat16), preferred_element_type=jnp.float32)
        cols = pl.ds(c * 256, 256)
        for b in range(FOLD // 16):
            r0, r1, r2, r3 = [sections[c, r, pl.ds(b * 16, 16), :] for r in range(RADIX)]
            i0, i1, i2, i3 = [sections[c, r, pl.ds(FOLD + b * 16, 16), :] for r in range(RADIX)]
            ar, ai, br, bi = r0 + r2, i0 + i2, r0 - r2, i0 - i2
            cr, ci, dr, di = r1 + r3, i1 + i3, i3 - i1, r1 - r3
            quarters = (
                (ar + cr, ai + ci), (br + dr, bi + di), (ar - cr, ai - ci), (br - dr, bi - di)
            )
            for q, (sr, si) in enumerate(quarters):
                rows = pl.ds(q * FOLD + b * 16, 16)
                tc, ts = twiddle[0, rows, cols], twiddle[1, rows, cols]
                twisted[0, rows, cols] = (sr * tc - si * ts).astype(jnp.bfloat16)
                twisted[1, rows, cols] = (sr * ts + si * tc).astype(jnp.bfloat16)
    ac = jnp.dot(twisted[0], second[...], preferred_element_type=jnp.float32)
    db = jnp.dot(twisted[1], second[...], preferred_element_type=jnp.float32)
    a, c, d, b = ac[:, :HALF], ac[:, HALF:], db[:, :HALF], db[:, HALF:]
    ad, bc = a * a + d * d, b * b + c * c
    both, cross = ad + bc, c * d - a * b
    edge = lax.broadcasted_iota(jnp.int32, (ROWS, LANES), 1) == 0
    low, high = pl.ds(0, LANES), pl.ds(LANES, HALF - LANES)
    total_q[:, low] += jnp.where(edge, 0.5 * both[:, :LANES], both[:, :LANES])
    total_q[:, high] += both[:, LANES:]
    total_r[:, low] += jnp.where(edge, 0.25 * (ad[:, :LANES] - bc[:, :LANES]), cross[:, :LANES])
    total_r[:, high] += cross[:, LANES:]


def largest(total_q, total_r):
    def body(i, acc):
        rows = pl.ds(pl.multiple_of(i * 32, 32), 32)
        return jnp.maximum(acc, total_q[rows, :] + 2.0 * jnp.abs(total_r[rows, :]))

    return jnp.max(lax.fori_loop(0, ROWS // 32, body, jnp.zeros((32, HALF), jnp.float32)))


def body(strain_slots, templates, cutoffs, lists, owner, slides):
    n, groups = lax.axis_size("tpl"), lax.axis_size("grp")
    bits = n.bit_length() - 2
    dets, bins = strain_slots.shape[1], strain_slots.shape[3]
    units, half = dets * CUT, bins // LANES // CUT
    strain = strain_slots[0].reshape(dets, 2, bins // LANES, LANES).transpose(0, 2, 1, 3)
    strain = strain.reshape(2 * units, half, LANES)
    count, shard = templates.shape[0], templates.shape[2]
    bank = templates.reshape(count, 2, shard // LANES, LANES).transpose(0, 2, 1, 3)
    bank = bank.reshape(count, 2 * shard // LANES, LANES)
    slots = lists.shape[1]
    first, twiddle, second = constant_tables()
    smem = pl.BlockSpec(memory_space=pltpu.SMEM)
    hbm = pl.BlockSpec(memory_space=pltpu.HBM)
    dma, bf16, f32 = pltpu.SemaphoreType.DMA, jnp.bfloat16, jnp.float32
    hrow = bank.shape[1] // groups
    results = pl.pallas_call(
        kernel,
        out_shape=jax.ShapeDtypeStruct((2 * slots,), f32),
        in_specs=[smem] * 4 + [hbm] * 5,
        out_specs=smem,
        scratch_shapes=[
            pltpu.VMEM((units, half, LANES), bf16),
            pltpu.VMEM((units, half, LANES), bf16),
            pltpu.VMEM((units, half, LANES), bf16),
            pltpu.VMEM((2 * units, half, LANES), bf16),
            pltpu.VMEM(bank.shape, bf16),
            pltpu.VMEM((slots, n, hrow, LANES), bf16),
            pltpu.VMEM((slots, n, bank.shape[1], LANES), bf16),
            pltpu.VMEM((TALL, LANES), f32),
            pltpu.VMEM((dets, 2, FOLD, LANES), f32),
            pltpu.VMEM((dets, 2, 8, WIDE), f32),
            pltpu.VMEM((dets, 2, FOLD, WIDE), f32),
            pltpu.VMEM((slots, 2, FOLD, WIDE), f32),
            pltpu.VMEM((2, ROWS, COLS), bf16),
            pltpu.VMEM((COLS // 256, RADIX, 2 * FOLD, 256), f32),
            pltpu.VMEM((slots, ROWS, HALF), f32),
            pltpu.VMEM((slots, ROWS, HALF), f32),
            pltpu.VMEM((slots, 8, LANES), f32),
            pltpu.VMEM(first.shape, bf16),
            pltpu.VMEM(twiddle.shape, f32),
            pltpu.VMEM(second.shape, bf16),
            dma((5 + units,)),
            pltpu.SemaphoreType.REGULAR((bits,)),
            dma, dma((units,)),
            dma, dma((bits, units)),
            dma, dma((bits, units)),
            dma, dma((2, units)),
            dma, dma((slots, n)),
            dma((max(1, groups - 1),)), dma((slots, max(1, groups - 1))),
        ],
        compiler_params=pltpu.CompilerParams(
            collective_id=0, has_side_effects=True, vmem_limit_bytes=56 * 1024 * 1024
        ),
        name="search",
    )(
        lists.T, owner, cutoffs, slides, strain, bank,
        jnp.asarray(first), jnp.asarray(twiddle), jnp.asarray(second),
    )
    return results[:slots], results[slots:]


def solution(mesh):
    in_specs = (
        P(("grp", "tpl"), None, None, None),
        P(None, None, "tpl"),
        P(),
        P(),
        P("grp"),
        P("grp"),
    )
    out_specs = (P(("grp", "tpl")), P(("grp", "tpl")))
    return jax.shard_map(body, mesh=mesh, in_specs=in_specs, out_specs=out_specs, check_vma=False)
```

```python
import functools

import jax
import jax.numpy as jnp
import numpy as np
from jax import lax
from jax.experimental import pallas as pl
from jax.experimental.pallas import tpu as pltpu
from jax.sharding import PartitionSpec as P

ROWS = 512
COLS = 512
RADIX = 4
FOLD = ROWS // RADIX
WIDE = RADIX * COLS
HALF = COLS // 2
LANES = 128
CHUNKS = WIDE // LANES
TALL = 2 * FOLD * CHUNKS

two_pi = 6.283185307179586
eps_norm = 1e-06

MESH = pl.DeviceIdType.MESH
CUT = 2
EARLY = 8
GAP = 1
PREPARE = 1
LATE_FROM = 2
LATE_STEP = 4
SWAP_STEP = 2
CROSS_STEP = 5
CROSS_FROM = 1


def use_chain(width, depth):
    return width == 2 and 2 <= depth <= 8


def turn_table(left_ids, right_ids, period):
    product_idx = left_ids[:, None] * right_ids[None, :] % period
    angles = product_idx.astype(np.float32) * np.float32(two_pi / period)
    return np.cos(angles), np.sin(angles)


def constant_tables():
    ids = np.arange(ROWS, dtype=np.int32)
    cos, sin = turn_table(ids[:FOLD], ids, ROWS)
    first = []
    for r in range(RADIX):
        c, s = cos[:, r::RADIX], sin[:, r::RADIX]
        first.append(np.concatenate([np.concatenate([c, -s], 1), np.concatenate([s, c], 1)], 0))
    twiddle = np.stack(turn_table(ids, ids, ROWS * COLS))
    cos, sin = turn_table(ids, ids[: HALF + 1], COLS)
    sin = sin[:, :HALF].copy()
    sin[:, 0] = cos[:, HALF]
    second = np.concatenate([cos[:, :HALF], sin], 1)
    return np.stack(first).astype(jnp.bfloat16), twiddle, second.astype(jnp.bfloat16)


def kernel(
    width, lists, owner, cutoffs, slides, strain, bank_hbm, first_hbm, twiddle_hbm, second_hbm,
    results,
    cand, other, heap, line, full, bank, picked, arrived, flat, row_phase, col_phase,
    turned, masked, twisted, sections, total_q, total_r, squares, first, twiddle, second,
    local_sem, near_sem, core_send, core_recv, rs_send, rs_recv, ag_send, ag_recv,
    line_send, line_recv, part_send, part_recv, swap_send, swap_recv, cross_send, cross_recv,
):
    n, groups = lax.axis_size("tpl"), lax.axis_size("grp")
    me, group = lax.axis_index("tpl"), lax.axis_index("grp")
    bits = n.bit_length() - 2
    depth = n // 2 // width
    chain = use_chain(width, depth)
    stages = 2 * depth if chain else 2 * bits
    core, chip = me % 2, me // 2
    dets = strain.shape[0] // (2 * CUT)
    units = dets * CUT
    half = strain.shape[1]
    slots = lists.shape[0]
    shard = bank.shape[1]
    hrow = shard // groups

    own_id = owner[0]
    own_chip = own_id // 2
    i_own = own_id == me

    bit = [chip // (1 << k) % 2 for k in range(bits)]
    base = [0]
    for k in range(bits):
        base.append(base[k] + bit[k] * (half >> (k + 1)))

    turns = [(1 << k) * (1 - 2 * (me // (1 << k) % 2)) for k in range(bits + 1)]

    def flip(mask):
        return me + sum(turns[k] for k in range(bits + 1) if mask >> k & 1)

    partner = flip(1)
    peers = [flip(2 << k) for k in range(bits)]

    def remote(src, dst, send, recv, **where):
        return pltpu.make_async_remote_copy(
            src_ref=src, dst_ref=dst, send_sem=send, recv_sem=recv, device_id=where, device_id_type=MESH
        )

    def rows(start, size):
        return pl.ds(pl.multiple_of(start, 16), size)

    def core_copy(u):
        return remote(strain.at[2 * u + 1 - core], other.at[u], core_send, core_recv.at[u], tpl=partner)

    def away(k):
        size = half >> (k + 1)
        return rows(base[k] + (1 - bit[k]) * size, size)

    def kept(k):
        return rows(base[k], half >> k)

    def pile(k):
        return pl.ds(half - (half >> k), half >> (k + 1))

    def rs_copy(u, k):
        return remote(
            cand.at[u, away(k)], heap.at[u, pile(k)], rs_send, rs_recv.at[k, u], tpl=peers[k]
        )

    def ag_copy(u, k):
        at = full.at[2 * u + core, kept(k + 1)]
        return remote(at, at, ag_send, ag_recv.at[k, u], tpl=peers[k])

    def ag_arrival(u, k):
        at = full.at[2 * u + core, away(k)]
        return remote(at, at, ag_send, ag_recv.at[k, u], tpl=peers[k])

    def part_copy(u, cc, which):
        at = full.at[2 * u + cc, kept(1) if which == 0 else away(0)]
        return remote(at, at, part_send, part_recv.at[which, u], tpl=partner)

    def swap_copy(slot, i):
        to = flip(i)
        return remote(
            picked.at[slot, to], arrived.at[slot, me, rows(group * hrow, hrow)],
            swap_send, swap_recv.at[slot, i], tpl=to,
        )

    def swap_arrival(slot, i):
        source = flip(i)
        return remote(
            picked.at[slot, me], arrived.at[slot, source, rows(group * hrow, hrow)],
            swap_send, swap_recv.at[slot, i], tpl=source,
        )

    def cross_copy(slot, i, g):
        at = arrived.at[slot, flip(i), rows(group * hrow, hrow)]
        return remote(
            at, at, cross_send.at[g - 1], cross_recv.at[slot, g - 1], grp=(group + g) % groups
        )

    def cross_arrivals(slot, g):
        at = picked.at[slot, pl.ds(0, n - 1)]
        return remote(
            at, at, cross_send.at[g - 1], cross_recv.at[slot, g - 1], grp=(group + g) % groups
        )

    tables = [
        pltpu.make_async_copy(first_hbm, first, local_sem.at[2]),
        pltpu.make_async_copy(twiddle_hbm, twiddle, local_sem.at[3]),
        pltpu.make_async_copy(second_hbm, second, local_sem.at[4]),
    ]
    mine_copies = [
        pltpu.make_async_copy(strain.at[2 * u + core], cand.at[u], local_sem.at[5 + u]) for u in range(units)
    ]
    bank_copy = pltpu.make_async_copy(bank_hbm, bank, local_sem.at[0])
    for copy in mine_copies:
        copy.start()
    bank_copy.start()

    barrier = pltpu.get_barrier_semaphore()
    for peer in [partner] + peers:
        pl.semaphore_signal(barrier, inc=1, device_id={"tpl": peer}, device_id_type=MESH)
    for g in range(1, groups):
        pl.semaphore_signal(barrier, inc=1, device_id={"grp": (group + g) % groups}, device_id_type=MESH)
    pl.semaphore_wait(barrier, bits + groups)

    for u in range(units):
        core_copy(u).start()

    def greet(k):
        pl.semaphore_signal(near_sem.at[k], inc=1, device_id={"tpl": ([partner] + peers)[k]}, device_id_type=MESH)

    def choice(u, where):
        cand[u, where] = jnp.where(i_own, cand[u, where], other[u, where])

    greet(0)
    for k in range(bits):
        pl.semaphore_wait(near_sem.at[k], 1)
        if k + 1 < bits:
            greet(k + 1)

    def open_unit(u):
        mine_copies[u].wait()
        core_copy(u).wait_recv()
        choice(u, away(0))
        rs_copy(u, 0).start()
        choice(u, kept(1))

    open_unit(0)
    bank_copy.wait()
    apart = sorted(range(2, n), key=lambda i: (i & 2, -i))
    alone = sum(1 for i in apart if not i & 2)
    queue = [(slot, 1) for slot in range(slots)]
    queue += [(slot, i) for slot in range(slots) for i in apart[:alone]]
    queue += [(slot, i) for slot in range(slots) for i in apart[alone:]]
    early = max(0, min(EARLY, len(queue)))

    def swap_start(q):
        slot, i = queue[q]
        to = flip(i)
        picked[slot, to] = bank[lists[slot, to], rows(group * hrow, hrow)]
        swap_copy(slot, i).start()

    def cross_start(q):
        slot, i = queue[q]
        swap_arrival(slot, i).wait_recv()
        for g in range(1, groups):
            cross_copy(slot, i, g).start()

    for q in range(early):
        swap_start(q)
    for u in range(1, units):
        open_unit(u)
    for copy in tables:
        copy.start()
    def merge(u, k, where, start, size):
        agree = own_chip // (1 << k) == chip // (1 << k)
        offset = half - (half >> k) + start - base[k + 1]
        return jnp.where(agree, cand[u, where], heap[u, rows(offset, size)])

    piece = half // (width * depth)
    z = chip // width
    near = me % (2 * width)
    onward = (jnp.minimum(z + 1, depth - 1) * 2 * width + near, jnp.maximum(z - 1, 0) * 2 * width + near)

    def strip(j):
        return rows(bit[0] * (half // 2) + j * piece, piece)

    def pane(j):
        return rows(j * piece, piece)

    def line_copy(way, u, j, first=False):
        src = cand.at[u, strip(j)] if first else line.at[way, u, pane(j)]
        return remote(
            src, line.at[way, u, pane(j)], line_send, line_recv.at[way, u, j], tpl=onward[way]
        )

    def spread_copy(way, u, j):
        at = full.at[2 * u + core, strip(j)]
        return remote(at, at, ag_send, ag_recv.at[u, j], tpl=onward[way])

    def hand_copy(u, j):
        at = full.at[2 * u + core, strip(j)]
        return remote(at, at, rs_send, rs_recv.at[1, u], tpl=peers[0])

    def chain_stage(u, e):
        line_owns = own_chip // width == z
        if e == 0:
            rs_copy(u, 0).wait_recv()
            cand[u, kept(1)] = merge(u, 0, kept(1), base[1], half // 2)
        if e < depth - 1:
            for way in range(2):
                behind = z if way == 0 else depth - 1 - z
                j = depth - 1 - e + z if way == 0 else e - (depth - 1 - z)

                @pl.when(behind == 0)
                def _():
                    line_copy(way, u, depth - 1 - e if way == 0 else e, True).start()

                if e > 0:
                    @pl.when((behind > 0) & (behind <= e))
                    def _():
                        line_copy(way, u, j).wait_recv()
                        line[way, u, pane(j)] = jnp.where(line_owns, cand[u, strip(j)], line[way, u, pane(j)])
                        line_copy(way, u, j).start()
        elif e == depth - 1:
            value = cand[u, strip(z)]

            @pl.when(z == 0)
            def _():
                line_copy(1, u, z).wait_recv()
                full[2 * u + core, strip(z)] = jnp.where(line_owns, value, line[1, u, pane(z)])
                spread_copy(0, u, z).start()

            @pl.when(z == depth - 1)
            def _():
                line_copy(0, u, z).wait_recv()
                full[2 * u + core, strip(z)] = jnp.where(line_owns, value, line[0, u, pane(z)])
                spread_copy(1, u, z).start()

            @pl.when((z > 0) & (z < depth - 1))
            def _():
                line_copy(0, u, z).wait_recv()
                line_copy(1, u, z).wait_recv()
                other_side = jnp.where(own_chip // width < z, line[0, u, pane(z)], line[1, u, pane(z)])
                full[2 * u + core, strip(z)] = jnp.where(line_owns, value, other_side)
                spread_copy(0, u, z).start()
                spread_copy(1, u, z).start()

            hand_copy(u, z).start()
        elif e < 2 * depth - 1:
            h = e - (depth - 1)
            for way in range(2):
                j = z - h if way == 0 else z + h
                ahead = depth - 1 - z if way == 0 else z

                @pl.when(z >= h if way == 0 else z + h < depth)
                def _():
                    spread_copy(way, u, j).wait_recv()

                    @pl.when(ahead > 0)
                    def _():
                        spread_copy(way, u, j).start()

                    hand_copy(u, j).start()
            if h == depth - 1:
                part_copy(u, core, 0).start()
        else:
            at = full.at[2 * u + core, away(0)]
            remote(at, at, rs_send, rs_recv.at[1, u], tpl=peers[0]).wait_recv()
            part_copy(u, core, 1).start()

    def stage(u, e):
        if chain:
            chain_stage(u, e)
        elif e < bits:
            k = e
            rs_copy(u, k).wait_recv()
            if k + 1 < bits:
                size = half >> (k + 2)
                start = base[k + 1] + (1 - bit[k + 1]) * size
                cand[u, away(k + 1)] = merge(u, k, away(k + 1), start, size)
                rs_copy(u, k + 1).start()
                cand[u, kept(k + 2)] = merge(u, k, kept(k + 2), base[k + 2], size)
            else:
                full[2 * u + core, kept(bits)] = merge(u, k, kept(bits), base[bits], half >> bits)
                ag_copy(u, bits - 1).start()
        else:
            k = 2 * bits - 1 - e
            ag_arrival(u, k).wait_recv()
            if k > 0:
                ag_copy(u, k - 1).start()
            if k < 2:
                part_copy(u, core, 1 - k).start()

    opening = [u + (GAP if chain and u // CUT == dets - 1 else 0) for u in range(units)]
    talk = opening[-1] + stages
    swap_step = SWAP_STEP if chain else max(SWAP_STEP, -(-(len(queue) - early) // (talk - 3)))
    cross_step = max(CROSS_STEP, -(-len(queue) // (talk - CROSS_FROM)))
    steps_of = [swap_step if t < LATE_FROM or not chain else LATE_STEP for t in range(talk)]
    starts = [min(len(queue), early + sum(steps_of[:t])) for t in range(talk + 1)]
    swap_slots = [range(starts[t], starts[t + 1]) for t in range(talk)]
    ends = [min(len(queue), (t - CROSS_FROM + 1) * cross_step, starts[max(0, t - 1)]) for t in range(talk)]
    ends = [max(0, end) if t >= CROSS_FROM else 0 for t, end in enumerate(ends)] + [len(queue)]
    cross_slots = [range(ends[t - 1] if t else 0, ends[t]) for t in range(talk + 1)]
    swap_slots.append(())
    talk += 1
    landed = [
        max(t for t in range(talk) if any(queue[q][0] == slot for q in cross_slots[t])) for slot in range(slots)
    ]
    turn_at = [at + stages for at in opening]
    mask_at = [at + 1 for at in landed]
    pairs = sorted(
        (max(turn_at[CUT * (d + 1) - 1], mask_at[slot]), d, slot) for d in range(dets) for slot in range(slots)
    )
    filter_at = [ready for ready, _, _ in pairs]
    if chain:
        for f in range(1, len(pairs)):
            filter_at[f] = max(filter_at[f], min(filter_at[f - 1] + 1, talk - 1))
    steps = max(filter_at[-1], talk, landed[-1]) + 1

    def choose(t, pairs):
        value, hit = 0, False
        for at, v in pairs:
            value, hit = jnp.where(t == at, v, value), (t == at) | hit
        return value, hit

    def step_body(t, _):
        for at in range(talk):
            @pl.when(t == at)
            def _():
                for e in range(stages):
                    if at - e in opening:
                        stage(opening.index(at - e), e)
                for q in cross_slots[at]:
                    cross_start(q)
                for q in swap_slots[at]:
                    swap_start(q)

        @pl.when(t == PREPARE)
        def _():
            make_phases(slides, row_phase, col_phase)
            for slot in range(slots):
                arrived[slot, me] = bank[lists[slot, me]]
            total_q[...] = jnp.zeros_like(total_q)
            total_r[...] = jnp.zeros_like(total_r)
            for copy in tables:
                copy.wait()

        u, now = choose(t, list(zip(turn_at, range(units))))

        @pl.when(now)
        def _():
            for which in range(2):
                part_arrival(u, which).wait_recv()
            turn_unit(full.at[pl.ds(2 * u, 2)], flat, row_phase, col_phase, turned, u // CUT, u % CUT)

        slot, now = choose(t, list(zip(mask_at, range(slots))))

        @pl.when(now)
        def _():
            for g in range(1, groups):
                cross_arrivals(slot, g).wait_recv()
            cutoff = cutoffs[lists[slot, me]]
            squares[slot] = mask_template(cutoff, arrived.at[slot], flat, masked.at[slot])

        def one_filter(f, _):
            slot = choose(f, [(k, pair[2]) for k, pair in enumerate(pairs)])[0]
            d = choose(f, [(k, pair[1]) for k, pair in enumerate(pairs)])[0]
            filter_detector(
                turned.at[d], masked.at[slot], first, twiddle, second, twisted, sections,
                total_q.at[slot], total_r.at[slot],
            )
            return 0

        begin = sum((t > at).astype(jnp.int32) for at in filter_at)
        end = sum((t >= at).astype(jnp.int32) for at in filter_at)
        lax.fori_loop(begin, end, one_filter, 0)
        return 0

    def part_arrival(u, which):
        at = full.at[2 * u + 1 - core, kept(1) if which == 0 else away(0)]
        return remote(at, at, part_send, part_recv.at[which, u], tpl=partner)

    lax.fori_loop(0, steps, step_body, 0)

    def sent(at, semaphore):
        remote(at, at, semaphore, core_recv.at[0], tpl=partner).wait_send()

    walk = heap.at[:, pl.ds(0, half - (half >> bits))]
    if chain:
        sent(other, rs_send)
        sent(other.at[:, pl.ds(0, (depth - 1) * piece)], line_send)
        inner = (z > 0) & (z < depth - 1)

        @pl.when(inner)
        def _():
            sent(other.at[:, pl.ds(0, (depth + 1) * piece)], ag_send)

        @pl.when(jnp.logical_not(inner))
        def _():
            sent(other.at[:, pl.ds(0, piece)], ag_send)
    else:
        sent(walk, rs_send)
        sent(walk, ag_send)
    for at, semaphore in (
        (other, core_send), (other, part_send), (picked.at[:, pl.ds(0, n - 1)], swap_send),
    ):
        sent(at, semaphore)
    for g in range(1, groups):
        sent(picked.at[:, pl.ds(0, n - 1)], cross_send.at[g - 1])
    for slot in range(slots):
        sigmasq = jnp.sum(squares[slot])
        results[slot] = largest(total_q.at[slot], total_r.at[slot]) / (2.0 * (sigmasq + eps_norm))
        results[slots + slot] = sigmasq / (ROWS * COLS)


def make_phases(slides, row_phase, col_phase):
    total = ROWS * COLS

    def body(d, _):
        slide = slides[d]
        row = lax.broadcasted_iota(jnp.int32, (FOLD, LANES), 0) * slide % FOLD
        row = row.astype(jnp.float32) * (two_pi / FOLD)
        row_phase[d, 0] = jnp.cos(row)
        row_phase[d, 1] = jnp.sin(row)
        col = lax.broadcasted_iota(jnp.int32, (8, WIDE), 1) * slide % total
        col = col.astype(jnp.float32) * (two_pi / total)
        col_phase[d, 0] = jnp.cos(col)
        col_phase[d, 1] = jnp.sin(col)
        return 0

    lax.fori_loop(0, row_phase.shape[0], body, 0)


def tile(flat, i, c, part):
    return flat[pl.ds((i * 8 * CHUNKS + c) * 2 + part, 8, stride=2 * CHUNKS), :]


def turn_unit(source, flat, row_phase, col_phase, turned, d, q):
    half, size = source.shape[1], 256
    high = FOLD // CUT

    def widen(i, _):
        for h in range(2):
            at = pl.ds(pl.multiple_of(i * size, size), size)
            flat[pl.ds(pl.multiple_of(h * half + i * size, size), size), :] = source[h, at, :].astype(jnp.float32)
        return 0

    lax.fori_loop(0, half // size, widen, 0)

    def body(i, _):
        at = pl.ds(pl.multiple_of(q * high + i * 8, 8), 8)
        rr, ri = row_phase[d, 0, at, :], row_phase[d, 1, at, :]
        for c in range(CHUNKS):
            cols = pl.ds(c * LANES, LANES)
            cr, ci = col_phase[d, 0, :, cols], col_phase[d, 1, :, cols]
            pr, pi = rr * cr - ri * ci, rr * ci + ri * cr
            xr, xi = tile(flat, i, c, 0), tile(flat, i, c, 1)
            turned[d, 0, at, cols] = xr * pr - xi * pi
            turned[d, 1, at, cols] = xr * pi + xi * pr
        return 0

    lax.fori_loop(0, high // 8, body, 0)


def mask_template(cutoff, source, flat, masked):
    shards, shard = source.shape[0], source.shape[1]

    def body(i, _):
        flat[pl.ds(pl.multiple_of(i * shard, shard), shard), :] = source[i].astype(jnp.float32)
        return 0

    lax.fori_loop(0, shards, body, 0)

    def mask(i, acc):
        at = pl.ds(pl.multiple_of(i * 8, 8), 8)
        base = (lax.broadcasted_iota(jnp.int32, (8, LANES), 0) + i * 8) * WIDE + lax.broadcasted_iota(
            jnp.int32, (8, LANES), 1
        )
        for c in range(CHUNKS):
            cols = pl.ds(c * LANES, LANES)
            inside = base < cutoff - c * LANES
            wr = jnp.where(inside, tile(flat, i, c, 0), 0.0)
            wi = jnp.where(inside, tile(flat, i, c, 1), 0.0)
            masked[0, at, cols] = wr
            masked[1, at, cols] = wi
            acc = acc + (wr * wr + wi * wi)
        return acc

    return lax.fori_loop(0, FOLD // 8, mask, jnp.zeros((8, LANES), jnp.float32))


def filter_detector(turned, masked, first, twiddle, second, twisted, sections, total_q, total_r):
    for c in range(COLS // 256):
        for r in range(RADIX):
            cols = pl.ds(r * COLS + c * 256, 256)
            xr, xi = turned[0, :, cols], turned[1, :, cols]
            wr, wi = masked[0, :, cols], masked[1, :, cols]
            product = jnp.concatenate([xr * wr + xi * wi, xi * wr - xr * wi], 0)
            sections[c, r] = jnp.dot(first[r], product.astype(jnp.bfloat16), preferred_element_type=jnp.float32)
        cols = pl.ds(c * 256, 256)
        for b in range(FOLD // 16):
            r0, r1, r2, r3 = [sections[c, r, pl.ds(b * 16, 16), :] for r in range(RADIX)]
            i0, i1, i2, i3 = [sections[c, r, pl.ds(FOLD + b * 16, 16), :] for r in range(RADIX)]
            ar, ai, br, bi = r0 + r2, i0 + i2, r0 - r2, i0 - i2
            cr, ci, dr, di = r1 + r3, i1 + i3, i3 - i1, r1 - r3
            quarters = (
                (ar + cr, ai + ci), (br + dr, bi + di), (ar - cr, ai - ci), (br - dr, bi - di)
            )
            for q, (sr, si) in enumerate(quarters):
                rows = pl.ds(q * FOLD + b * 16, 16)
                tc, ts = twiddle[0, rows, cols], twiddle[1, rows, cols]
                twisted[0, rows, cols] = (sr * tc - si * ts).astype(jnp.bfloat16)
                twisted[1, rows, cols] = (sr * ts + si * tc).astype(jnp.bfloat16)
    ac = jnp.dot(twisted[0], second[...], preferred_element_type=jnp.float32)
    db = jnp.dot(twisted[1], second[...], preferred_element_type=jnp.float32)
    a, c, d, b = ac[:, :HALF], ac[:, HALF:], db[:, :HALF], db[:, HALF:]
    ad, bc = a * a + d * d, b * b + c * c
    both, cross = ad + bc, c * d - a * b
    edge = lax.broadcasted_iota(jnp.int32, (ROWS, LANES), 1) == 0
    low, high = pl.ds(0, LANES), pl.ds(LANES, HALF - LANES)
    total_q[:, low] += jnp.where(edge, 0.5 * both[:, :LANES], both[:, :LANES])
    total_q[:, high] += both[:, LANES:]
    total_r[:, low] += jnp.where(edge, 0.25 * (ad[:, :LANES] - bc[:, :LANES]), cross[:, :LANES])
    total_r[:, high] += cross[:, LANES:]


def largest(total_q, total_r):
    def body(i, acc):
        rows = pl.ds(pl.multiple_of(i * 32, 32), 32)
        return jnp.maximum(acc, total_q[rows, :] + 2.0 * jnp.abs(total_r[rows, :]))

    return jnp.max(lax.fori_loop(0, ROWS // 32, body, jnp.zeros((32, HALF), jnp.float32)))


def body(width, strain_slots, templates, cutoffs, lists, owner, slides):
    n, groups = lax.axis_size("tpl"), lax.axis_size("grp")
    bits = n.bit_length() - 2
    depth = n // 2 // width
    chain = use_chain(width, depth)
    dets, bins = strain_slots.shape[1], strain_slots.shape[3]
    units, half = dets * CUT, bins // LANES // CUT
    strain = strain_slots[0].reshape(dets, 2, bins // LANES, LANES).transpose(0, 2, 1, 3)
    strain = strain.reshape(2 * units, half, LANES)
    count, shard = templates.shape[0], templates.shape[2]
    bank = templates.reshape(count, 2, shard // LANES, LANES).transpose(0, 2, 1, 3)
    bank = bank.reshape(count, 2 * shard // LANES, LANES)
    slots = lists.shape[1]
    first, twiddle, second = constant_tables()
    smem = pl.BlockSpec(memory_space=pltpu.SMEM)
    hbm = pl.BlockSpec(memory_space=pltpu.HBM)
    dma, bf16, f32 = pltpu.SemaphoreType.DMA, jnp.bfloat16, jnp.float32
    hrow = bank.shape[1] // groups
    results = pl.pallas_call(
        functools.partial(kernel, width),
        out_shape=jax.ShapeDtypeStruct((2 * slots,), f32),
        in_specs=[smem] * 4 + [hbm] * 5,
        out_specs=smem,
        scratch_shapes=[
            pltpu.VMEM((units, half, LANES), bf16),
            pltpu.VMEM((units, half, LANES), bf16),
            pltpu.VMEM((units, half, LANES), bf16),
            pltpu.VMEM((2, units, half // width, LANES) if chain else (8, LANES), bf16),
            pltpu.VMEM((2 * units, half, LANES), bf16),
            pltpu.VMEM(bank.shape, bf16),
            pltpu.VMEM((slots, n, hrow, LANES), bf16),
            pltpu.VMEM((slots, n, bank.shape[1], LANES), bf16),
            pltpu.VMEM((TALL, LANES), f32),
            pltpu.VMEM((dets, 2, FOLD, LANES), f32),
            pltpu.VMEM((dets, 2, 8, WIDE), f32),
            pltpu.VMEM((dets, 2, FOLD, WIDE), f32),
            pltpu.VMEM((slots, 2, FOLD, WIDE), f32),
            pltpu.VMEM((2, ROWS, COLS), bf16),
            pltpu.VMEM((COLS // 256, RADIX, 2 * FOLD, 256), f32),
            pltpu.VMEM((slots, ROWS, HALF), f32),
            pltpu.VMEM((slots, ROWS, HALF), f32),
            pltpu.VMEM((slots, 8, LANES), f32),
            pltpu.VMEM(first.shape, bf16),
            pltpu.VMEM(twiddle.shape, f32),
            pltpu.VMEM(second.shape, bf16),
            dma((5 + units,)),
            pltpu.SemaphoreType.REGULAR((bits,)),
            dma, dma((units,)),
            dma, dma((bits, units)),
            dma, dma((units, depth) if chain else (bits, units)),
            dma, dma((2, units, depth) if chain else (1,)),
            dma, dma((2, units)),
            dma, dma((slots, n)),
            dma((max(1, groups - 1),)), dma((slots, max(1, groups - 1))),
        ],
        compiler_params=pltpu.CompilerParams(
            collective_id=0, has_side_effects=True, vmem_limit_bytes=56 * 1024 * 1024
        ),
        name="search",
    )(
        lists.T, owner, cutoffs, slides, strain, bank,
        jnp.asarray(first), jnp.asarray(twiddle), jnp.asarray(second),
    )
    return results[:slots], results[slots:]


def solution(mesh):
    in_specs = (
        P(("grp", "tpl"), None, None, None),
        P(None, None, "tpl"),
        P(),
        P(),
        P("grp"),
        P("grp"),
    )
    out_specs = (P(("grp", "tpl")), P(("grp", "tpl")))
    width = len({d.coords[1] for d in mesh.devices[0].flat})
    body_of = functools.partial(body, width)
    return jax.shard_map(body_of, mesh=mesh, in_specs=in_specs, out_specs=out_specs, check_vma=False)
```

```python
import functools

import jax
import jax.numpy as jnp
import numpy as np
from jax import lax
from jax.experimental import pallas as pl
from jax.experimental.pallas import tpu as pltpu
from jax.sharding import PartitionSpec as P

ROWS = 512
COLS = 512
RADIX = 4
FOLD = ROWS // RADIX
WIDE = RADIX * COLS
HALF = COLS // 2
LANES = 128
CHUNKS = WIDE // LANES
PITCH = 2 * CHUNKS + 8
TALL = FOLD * PITCH

two_pi = 6.283185307179586
eps_norm = 1e-06

MESH = pl.DeviceIdType.MESH
CUT = 2
EARLY = 8
GAP = 1
PREPARE = 1
LATE_FROM = 2
LATE_STEP = 4
SWAP_STEP = 2
CROSS_STEP = 5
CROSS_FROM = 1


def use_chain(width, depth):
    return width == 2 and 2 <= depth <= 8


def turn_table(left_ids, right_ids, period):
    product_idx = left_ids[:, None] * right_ids[None, :] % period
    angles = product_idx.astype(np.float32) * np.float32(two_pi / period)
    return np.cos(angles), np.sin(angles)


def constant_tables():
    ids = np.arange(ROWS, dtype=np.int32)
    cos, sin = turn_table(ids[:FOLD], ids, ROWS)
    first = []
    for r in range(RADIX):
        c, s = cos[:, r::RADIX], sin[:, r::RADIX]
        first.append(np.concatenate([np.concatenate([c, -s], 1), np.concatenate([s, c], 1)], 0))
    twiddle = np.stack(turn_table(ids, ids, ROWS * COLS))
    cos, sin = turn_table(ids, ids[: HALF + 1], COLS)
    sin = sin[:, :HALF].copy()
    sin[:, 0] = cos[:, HALF]
    second = np.concatenate([cos[:, :HALF], sin], 1)
    return np.stack(first).astype(jnp.bfloat16), twiddle, second.astype(jnp.bfloat16)


def kernel(
    width, lists, owner, cutoffs, slides, strain, bank_hbm, first_hbm, twiddle_hbm, second_hbm,
    results,
    cand, other, heap, line, full, bank, picked, arrived, flat, row_phase, col_phase,
    turned, masked, twisted, sections, total_q, total_r, squares, first, twiddle, second,
    local_sem, near_sem, core_send, core_recv, rs_send, rs_recv, ag_send, ag_recv,
    line_send, line_recv, part_send, part_recv, swap_send, swap_recv, cross_send, cross_recv,
):
    n, groups = lax.axis_size("tpl"), lax.axis_size("grp")
    me, group = lax.axis_index("tpl"), lax.axis_index("grp")
    bits = n.bit_length() - 2
    depth = n // 2 // width
    chain = use_chain(width, depth)
    stages = 2 * depth if chain else 2 * bits
    core, chip = me % 2, me // 2
    dets = strain.shape[0] // (2 * CUT)
    units = dets * CUT
    half = strain.shape[1]
    slots = lists.shape[0]
    shard = bank.shape[1]
    hrow = shard // groups

    own_id = owner[0]
    own_chip = own_id // 2
    i_own = own_id == me

    bit = [chip // (1 << k) % 2 for k in range(bits)]
    base = [0]
    for k in range(bits):
        base.append(base[k] + bit[k] * (half >> (k + 1)))

    turns = [(1 << k) * (1 - 2 * (me // (1 << k) % 2)) for k in range(bits + 1)]

    def flip(mask):
        return me + sum(turns[k] for k in range(bits + 1) if mask >> k & 1)

    partner = flip(1)
    peers = [flip(2 << k) for k in range(bits)]

    def remote(src, dst, send, recv, **where):
        return pltpu.make_async_remote_copy(
            src_ref=src, dst_ref=dst, send_sem=send, recv_sem=recv, device_id=where, device_id_type=MESH
        )

    def rows(start, size):
        return pl.ds(pl.multiple_of(start, 16), size)

    def core_copy(u):
        return remote(strain.at[2 * u + 1 - core], other.at[u], core_send, core_recv.at[u], tpl=partner)

    def away(k):
        size = half >> (k + 1)
        return rows(base[k] + (1 - bit[k]) * size, size)

    def kept(k):
        return rows(base[k], half >> k)

    def pile(k):
        return pl.ds(half - (half >> k), half >> (k + 1))

    def rs_copy(u, k):
        return remote(
            cand.at[u, away(k)], heap.at[u, pile(k)], rs_send, rs_recv.at[k, u], tpl=peers[k]
        )

    def ag_copy(u, k):
        at = full.at[2 * u + core, kept(k + 1)]
        return remote(at, at, ag_send, ag_recv.at[k, u], tpl=peers[k])

    def ag_arrival(u, k):
        at = full.at[2 * u + core, away(k)]
        return remote(at, at, ag_send, ag_recv.at[k, u], tpl=peers[k])

    def part_copy(u, cc, which):
        at = full.at[2 * u + cc, kept(1) if which == 0 else away(0)]
        return remote(at, at, part_send, part_recv.at[which, u], tpl=partner)

    def swap_copy(slot, i):
        to = flip(i)
        return remote(
            picked.at[slot, to], arrived.at[slot, me, rows(group * hrow, hrow)],
            swap_send, swap_recv.at[slot, i], tpl=to,
        )

    def swap_arrival(slot, i):
        source = flip(i)
        return remote(
            picked.at[slot, me], arrived.at[slot, source, rows(group * hrow, hrow)],
            swap_send, swap_recv.at[slot, i], tpl=source,
        )

    def cross_copy(slot, i, g):
        at = arrived.at[slot, flip(i), rows(group * hrow, hrow)]
        return remote(
            at, at, cross_send.at[g - 1], cross_recv.at[slot, g - 1], grp=(group + g) % groups
        )

    def cross_arrivals(slot, g):
        at = picked.at[slot, pl.ds(0, n - 1)]
        return remote(
            at, at, cross_send.at[g - 1], cross_recv.at[slot, g - 1], grp=(group + g) % groups
        )

    tables = [
        pltpu.make_async_copy(first_hbm, first, local_sem.at[2]),
        pltpu.make_async_copy(twiddle_hbm, twiddle, local_sem.at[3]),
        pltpu.make_async_copy(second_hbm, second, local_sem.at[4]),
    ]
    mine_copies = [
        pltpu.make_async_copy(strain.at[2 * u + core], cand.at[u], local_sem.at[5 + u]) for u in range(units)
    ]
    bank_copy = pltpu.make_async_copy(bank_hbm, bank, local_sem.at[0])
    for copy in mine_copies:
        copy.start()
    bank_copy.start()

    barrier = pltpu.get_barrier_semaphore()
    for peer in [partner] + peers:
        pl.semaphore_signal(barrier, inc=1, device_id={"tpl": peer}, device_id_type=MESH)
    for g in range(1, groups):
        pl.semaphore_signal(barrier, inc=1, device_id={"grp": (group + g) % groups}, device_id_type=MESH)
    pl.semaphore_wait(barrier, bits + groups)

    for u in range(units):
        core_copy(u).start()

    def greet(k):
        pl.semaphore_signal(near_sem.at[k], inc=1, device_id={"tpl": ([partner] + peers)[k]}, device_id_type=MESH)

    def choice(u, where):
        cand[u, where] = jnp.where(i_own, cand[u, where], other[u, where])

    greet(0)
    for k in range(bits):
        pl.semaphore_wait(near_sem.at[k], 1)
        if k + 1 < bits:
            greet(k + 1)

    def open_unit(u):
        mine_copies[u].wait()
        core_copy(u).wait_recv()
        choice(u, away(0))
        rs_copy(u, 0).start()
        choice(u, kept(1))

    open_unit(0)
    bank_copy.wait()
    apart = sorted(range(2, n), key=lambda i: (i & 2, -i))
    alone = sum(1 for i in apart if not i & 2)
    queue = [(slot, 1) for slot in range(slots)]
    queue += [(slot, i) for slot in range(slots) for i in apart[:alone]]
    queue += [(slot, i) for slot in range(slots) for i in apart[alone:]]
    early = max(0, min(EARLY, len(queue)))

    def swap_start(q):
        slot, i = queue[q]
        to = flip(i)
        picked[slot, to] = bank[lists[slot, to], rows(group * hrow, hrow)]
        swap_copy(slot, i).start()

    def cross_start(q):
        slot, i = queue[q]
        swap_arrival(slot, i).wait_recv()
        for g in range(1, groups):
            cross_copy(slot, i, g).start()

    for q in range(early):
        swap_start(q)
    for u in range(1, units):
        open_unit(u)
    for copy in tables:
        copy.start()
    def merge(u, k, where, start, size):
        agree = own_chip // (1 << k) == chip // (1 << k)
        offset = half - (half >> k) + start - base[k + 1]
        return jnp.where(agree, cand[u, where], heap[u, rows(offset, size)])

    piece = half // (width * depth)
    z = chip // width
    near = me % (2 * width)
    onward = (jnp.minimum(z + 1, depth - 1) * 2 * width + near, jnp.maximum(z - 1, 0) * 2 * width + near)

    def strip(j):
        return rows(bit[0] * (half // 2) + j * piece, piece)

    def pane(j):
        return rows(j * piece, piece)

    def line_copy(way, u, j, first=False):
        src = cand.at[u, strip(j)] if first else line.at[way, u, pane(j)]
        return remote(
            src, line.at[way, u, pane(j)], line_send, line_recv.at[way, u, j], tpl=onward[way]
        )

    def spread_copy(way, u, j):
        at = full.at[2 * u + core, strip(j)]
        return remote(at, at, ag_send, ag_recv.at[u, j], tpl=onward[way])

    def hand_copy(u, j):
        at = full.at[2 * u + core, strip(j)]
        return remote(at, at, rs_send, rs_recv.at[1, u], tpl=peers[0])

    def chain_stage(u, e):
        line_owns = own_chip // width == z
        if e == 0:
            rs_copy(u, 0).wait_recv()
            cand[u, kept(1)] = merge(u, 0, kept(1), base[1], half // 2)
        if e < depth - 1:
            for way in range(2):
                behind = z if way == 0 else depth - 1 - z
                j = depth - 1 - e + z if way == 0 else e - (depth - 1 - z)

                @pl.when(behind == 0)
                def _():
                    line_copy(way, u, depth - 1 - e if way == 0 else e, True).start()

                if e > 0:
                    @pl.when((behind > 0) & (behind <= e))
                    def _():
                        line_copy(way, u, j).wait_recv()
                        line[way, u, pane(j)] = jnp.where(line_owns, cand[u, strip(j)], line[way, u, pane(j)])
                        line_copy(way, u, j).start()
        elif e == depth - 1:
            value = cand[u, strip(z)]

            @pl.when(z == 0)
            def _():
                line_copy(1, u, z).wait_recv()
                full[2 * u + core, strip(z)] = jnp.where(line_owns, value, line[1, u, pane(z)])
                spread_copy(0, u, z).start()

            @pl.when(z == depth - 1)
            def _():
                line_copy(0, u, z).wait_recv()
                full[2 * u + core, strip(z)] = jnp.where(line_owns, value, line[0, u, pane(z)])
                spread_copy(1, u, z).start()

            @pl.when((z > 0) & (z < depth - 1))
            def _():
                line_copy(0, u, z).wait_recv()
                line_copy(1, u, z).wait_recv()
                other_side = jnp.where(own_chip // width < z, line[0, u, pane(z)], line[1, u, pane(z)])
                full[2 * u + core, strip(z)] = jnp.where(line_owns, value, other_side)
                spread_copy(0, u, z).start()
                spread_copy(1, u, z).start()

            hand_copy(u, z).start()
        elif e < 2 * depth - 1:
            h = e - (depth - 1)
            for way in range(2):
                j = z - h if way == 0 else z + h
                ahead = depth - 1 - z if way == 0 else z

                @pl.when(z >= h if way == 0 else z + h < depth)
                def _():
                    spread_copy(way, u, j).wait_recv()

                    @pl.when(ahead > 0)
                    def _():
                        spread_copy(way, u, j).start()

                    hand_copy(u, j).start()
            if h == depth - 1:
                part_copy(u, core, 0).start()
        else:
            at = full.at[2 * u + core, away(0)]
            remote(at, at, rs_send, rs_recv.at[1, u], tpl=peers[0]).wait_recv()
            part_copy(u, core, 1).start()

    def stage(u, e):
        if chain:
            chain_stage(u, e)
        elif e < bits:
            k = e
            rs_copy(u, k).wait_recv()
            if k + 1 < bits:
                size = half >> (k + 2)
                start = base[k + 1] + (1 - bit[k + 1]) * size
                cand[u, away(k + 1)] = merge(u, k, away(k + 1), start, size)
                rs_copy(u, k + 1).start()
                cand[u, kept(k + 2)] = merge(u, k, kept(k + 2), base[k + 2], size)
            else:
                full[2 * u + core, kept(bits)] = merge(u, k, kept(bits), base[bits], half >> bits)
                ag_copy(u, bits - 1).start()
        else:
            k = 2 * bits - 1 - e
            ag_arrival(u, k).wait_recv()
            if k > 0:
                ag_copy(u, k - 1).start()
            if k < 2:
                part_copy(u, core, 1 - k).start()

    opening = [u + (GAP if chain and u // CUT == dets - 1 else 0) for u in range(units)]
    talk = opening[-1] + stages
    swap_step = SWAP_STEP if chain else max(SWAP_STEP, -(-(len(queue) - early) // (talk - 3)))
    cross_step = max(CROSS_STEP, -(-len(queue) // (talk - CROSS_FROM)))
    steps_of = [swap_step if t < LATE_FROM or not chain else LATE_STEP for t in range(talk)]
    starts = [min(len(queue), early + sum(steps_of[:t])) for t in range(talk + 1)]
    swap_slots = [range(starts[t], starts[t + 1]) for t in range(talk)]
    ends = [min(len(queue), (t - CROSS_FROM + 1) * cross_step, starts[max(0, t - 1)]) for t in range(talk)]
    ends = [max(0, end) if t >= CROSS_FROM else 0 for t, end in enumerate(ends)] + [len(queue)]
    cross_slots = [range(ends[t - 1] if t else 0, ends[t]) for t in range(talk + 1)]
    swap_slots.append(())
    talk += 1
    landed = [
        max(t for t in range(talk) if any(queue[q][0] == slot for q in cross_slots[t])) for slot in range(slots)
    ]
    turn_at = [at + stages for at in opening]
    mask_at = [at + 1 for at in landed]
    pairs = sorted(
        (max(turn_at[CUT * (d + 1) - 1], mask_at[slot]), d, slot) for d in range(dets) for slot in range(slots)
    )
    filter_at = [ready for ready, _, _ in pairs]
    if chain:
        for f in range(1, len(pairs)):
            filter_at[f] = max(filter_at[f], min(filter_at[f - 1] + 1, talk - 1))
    steps = max(filter_at[-1], talk, landed[-1]) + 1

    def choose(t, pairs):
        value, hit = 0, False
        for at, v in pairs:
            value, hit = jnp.where(t == at, v, value), (t == at) | hit
        return value, hit

    def step_body(t, _):
        for at in range(talk):
            @pl.when(t == at)
            def _():
                for e in range(stages):
                    if at - e in opening:
                        stage(opening.index(at - e), e)
                for q in cross_slots[at]:
                    cross_start(q)
                for q in swap_slots[at]:
                    swap_start(q)

        @pl.when(t == PREPARE)
        def _():
            make_phases(slides, row_phase, col_phase)
            for slot in range(slots):
                arrived[slot, me] = bank[lists[slot, me]]
            total_q[...] = jnp.zeros_like(total_q)
            total_r[...] = jnp.zeros_like(total_r)
            for copy in tables:
                copy.wait()

        u, now = choose(t, list(zip(turn_at, range(units))))

        @pl.when(now)
        def _():
            for which in range(2):
                part_arrival(u, which).wait_recv()
            turn_unit(full.at[pl.ds(2 * u, 2)], flat, row_phase, col_phase, turned, u // CUT, u % CUT)

        slot, now = choose(t, list(zip(mask_at, range(slots))))

        @pl.when(now)
        def _():
            for g in range(1, groups):
                cross_arrivals(slot, g).wait_recv()
            cutoff = cutoffs[lists[slot, me]]
            squares[slot] = mask_template(cutoff, arrived.at[slot], flat, masked.at[slot])

        def one_filter(f, _):
            slot = choose(f, [(k, pair[2]) for k, pair in enumerate(pairs)])[0]
            d = choose(f, [(k, pair[1]) for k, pair in enumerate(pairs)])[0]
            filter_detector(
                turned.at[d], masked.at[slot], first, twiddle, second, twisted, sections,
                total_q.at[slot], total_r.at[slot],
            )
            return 0

        begin = sum((t > at).astype(jnp.int32) for at in filter_at)
        end = sum((t >= at).astype(jnp.int32) for at in filter_at)
        lax.fori_loop(begin, end, one_filter, 0)
        return 0

    def part_arrival(u, which):
        at = full.at[2 * u + 1 - core, kept(1) if which == 0 else away(0)]
        return remote(at, at, part_send, part_recv.at[which, u], tpl=partner)

    lax.fori_loop(0, steps, step_body, 0)

    def sent(at, semaphore):
        remote(at, at, semaphore, core_recv.at[0], tpl=partner).wait_send()

    walk = heap.at[:, pl.ds(0, half - (half >> bits))]
    if chain:
        sent(other, rs_send)
        sent(other.at[:, pl.ds(0, (depth - 1) * piece)], line_send)
        inner = (z > 0) & (z < depth - 1)

        @pl.when(inner)
        def _():
            sent(other.at[:, pl.ds(0, (depth + 1) * piece)], ag_send)

        @pl.when(jnp.logical_not(inner))
        def _():
            sent(other.at[:, pl.ds(0, piece)], ag_send)
    else:
        sent(walk, rs_send)
        sent(walk, ag_send)
    for at, semaphore in (
        (other, core_send), (other, part_send), (picked.at[:, pl.ds(0, n - 1)], swap_send),
    ):
        sent(at, semaphore)
    for g in range(1, groups):
        sent(picked.at[:, pl.ds(0, n - 1)], cross_send.at[g - 1])
    for slot in range(slots):
        sigmasq = jnp.sum(squares[slot])
        results[slot] = largest(total_q.at[slot], total_r.at[slot]) / (2.0 * (sigmasq + eps_norm))
        results[slots + slot] = sigmasq / (ROWS * COLS)


def make_phases(slides, row_phase, col_phase):
    total = ROWS * COLS

    def body(d, _):
        slide = slides[d]
        row = lax.broadcasted_iota(jnp.int32, (FOLD, LANES), 0) * slide % FOLD
        row = row.astype(jnp.float32) * (two_pi / FOLD)
        row_phase[d, 0] = jnp.cos(row)
        row_phase[d, 1] = jnp.sin(row)
        col = lax.broadcasted_iota(jnp.int32, (8, WIDE), 1) * slide % total
        col = col.astype(jnp.float32) * (two_pi / total)
        col_phase[d, 0] = jnp.cos(col)
        col_phase[d, 1] = jnp.sin(col)
        return 0

    lax.fori_loop(0, row_phase.shape[0], body, 0)


def tile(flat, i, c, part):
    return flat[pl.ds(i * 8 * PITCH + c * 2 + part, 8, stride=PITCH), :]


def turn_unit(source, flat, row_phase, col_phase, turned, d, q):
    half = source.shape[1]
    high = FOLD // CUT

    span = 2 * CHUNKS

    def widen(i, _):
        for h in range(2):
            for r in range(8):
                at = pl.ds(pl.multiple_of((i * 8 + r) * span, span), span)
                to = pl.ds(pl.multiple_of((h * (half // span) + i * 8 + r) * PITCH, 8), span)
                flat[to, :] = source[h, at, :].astype(jnp.float32)
        return 0

    lax.fori_loop(0, half // (8 * span), widen, 0)

    def body(i, _):
        at = pl.ds(pl.multiple_of(q * high + i * 8, 8), 8)
        rr, ri = row_phase[d, 0, at, :], row_phase[d, 1, at, :]
        for c in range(CHUNKS):
            cols = pl.ds(c * LANES, LANES)
            cr, ci = col_phase[d, 0, :, cols], col_phase[d, 1, :, cols]
            pr, pi = rr * cr - ri * ci, rr * ci + ri * cr
            xr, xi = tile(flat, i, c, 0), tile(flat, i, c, 1)
            turned[d, 0, at, cols] = xr * pr - xi * pi
            turned[d, 1, at, cols] = xr * pi + xi * pr
        return 0

    lax.fori_loop(0, high // 8, body, 0)


def mask_template(cutoff, source, flat, masked):
    shards, shard = source.shape[0], source.shape[1]

    def body(i, _):
        for r in range(shard // (2 * CHUNKS)):
            to = pl.ds(pl.multiple_of((i * (shard // (2 * CHUNKS)) + r) * PITCH, 8), 2 * CHUNKS)
            flat[to, :] = source[i, r * 2 * CHUNKS : (r + 1) * 2 * CHUNKS, :].astype(jnp.float32)
        return 0

    lax.fori_loop(0, shards, body, 0)

    def mask(i, acc):
        at = pl.ds(pl.multiple_of(i * 8, 8), 8)
        base = (lax.broadcasted_iota(jnp.int32, (8, LANES), 0) + i * 8) * WIDE + lax.broadcasted_iota(
            jnp.int32, (8, LANES), 1
        )
        for c in range(CHUNKS):
            cols = pl.ds(c * LANES, LANES)
            inside = base < cutoff - c * LANES
            wr = jnp.where(inside, tile(flat, i, c, 0), 0.0)
            wi = jnp.where(inside, tile(flat, i, c, 1), 0.0)
            masked[0, at, cols] = wr
            masked[1, at, cols] = wi
            acc = acc + (wr * wr + wi * wi)
        return acc

    return lax.fori_loop(0, FOLD // 8, mask, jnp.zeros((8, LANES), jnp.float32))


def filter_detector(turned, masked, first, twiddle, second, twisted, sections, total_q, total_r):
    for c in range(COLS // 256):
        for r in range(RADIX):
            cols = pl.ds(r * COLS + c * 256, 256)
            xr, xi = turned[0, :, cols], turned[1, :, cols]
            wr, wi = masked[0, :, cols], masked[1, :, cols]
            product = jnp.concatenate([xr * wr + xi * wi, xi * wr - xr * wi], 0)
            sections[c, r] = jnp.dot(first[r], product.astype(jnp.bfloat16), preferred_element_type=jnp.float32)
        cols = pl.ds(c * 256, 256)
        for b in range(FOLD // 16):
            r0, r1, r2, r3 = [sections[c, r, pl.ds(b * 16, 16), :] for r in range(RADIX)]
            i0, i1, i2, i3 = [sections[c, r, pl.ds(FOLD + b * 16, 16), :] for r in range(RADIX)]
            ar, ai, br, bi = r0 + r2, i0 + i2, r0 - r2, i0 - i2
            cr, ci, dr, di = r1 + r3, i1 + i3, i3 - i1, r1 - r3
            quarters = (
                (ar + cr, ai + ci), (br + dr, bi + di), (ar - cr, ai - ci), (br - dr, bi - di)
            )
            for q, (sr, si) in enumerate(quarters):
                rows = pl.ds(q * FOLD + b * 16, 16)
                tc, ts = twiddle[0, rows, cols], twiddle[1, rows, cols]
                twisted[0, rows, cols] = (sr * tc - si * ts).astype(jnp.bfloat16)
                twisted[1, rows, cols] = (sr * ts + si * tc).astype(jnp.bfloat16)
    ac = jnp.dot(twisted[0], second[...], preferred_element_type=jnp.float32)
    db = jnp.dot(twisted[1], second[...], preferred_element_type=jnp.float32)
    a, c, d, b = ac[:, :HALF], ac[:, HALF:], db[:, :HALF], db[:, HALF:]
    ad, bc = a * a + d * d, b * b + c * c
    both, cross = ad + bc, c * d - a * b
    edge = lax.broadcasted_iota(jnp.int32, (ROWS, LANES), 1) == 0
    low, high = pl.ds(0, LANES), pl.ds(LANES, HALF - LANES)
    total_q[:, low] += jnp.where(edge, 0.5 * both[:, :LANES], both[:, :LANES])
    total_q[:, high] += both[:, LANES:]
    total_r[:, low] += jnp.where(edge, 0.25 * (ad[:, :LANES] - bc[:, :LANES]), cross[:, :LANES])
    total_r[:, high] += cross[:, LANES:]


def largest(total_q, total_r):
    def body(i, acc):
        rows = pl.ds(pl.multiple_of(i * 32, 32), 32)
        return jnp.maximum(acc, total_q[rows, :] + 2.0 * jnp.abs(total_r[rows, :]))

    return jnp.max(lax.fori_loop(0, ROWS // 32, body, jnp.zeros((32, HALF), jnp.float32)))


def body(width, strain_slots, templates, cutoffs, lists, owner, slides):
    n, groups = lax.axis_size("tpl"), lax.axis_size("grp")
    bits = n.bit_length() - 2
    depth = n // 2 // width
    chain = use_chain(width, depth)
    dets, bins = strain_slots.shape[1], strain_slots.shape[3]
    units, half = dets * CUT, bins // LANES // CUT
    strain = strain_slots[0].reshape(dets, 2, bins // LANES, LANES).transpose(0, 2, 1, 3)
    strain = strain.reshape(2 * units, half, LANES)
    count, shard = templates.shape[0], templates.shape[2]
    bank = templates.reshape(count, 2, shard // LANES, LANES).transpose(0, 2, 1, 3)
    bank = bank.reshape(count, 2 * shard // LANES, LANES)
    slots = lists.shape[1]
    first, twiddle, second = constant_tables()
    smem = pl.BlockSpec(memory_space=pltpu.SMEM)
    hbm = pl.BlockSpec(memory_space=pltpu.HBM)
    dma, bf16, f32 = pltpu.SemaphoreType.DMA, jnp.bfloat16, jnp.float32
    hrow = bank.shape[1] // groups
    results = pl.pallas_call(
        functools.partial(kernel, width),
        out_shape=jax.ShapeDtypeStruct((2 * slots,), f32),
        in_specs=[smem] * 4 + [hbm] * 5,
        out_specs=smem,
        scratch_shapes=[
            pltpu.VMEM((units, half, LANES), bf16),
            pltpu.VMEM((units, half, LANES), bf16),
            pltpu.VMEM((units, half, LANES), bf16),
            pltpu.VMEM((2, units, half // width, LANES) if chain else (8, LANES), bf16),
            pltpu.VMEM((2 * units, half, LANES), bf16),
            pltpu.VMEM(bank.shape, bf16),
            pltpu.VMEM((slots, n, hrow, LANES), bf16),
            pltpu.VMEM((slots, n, bank.shape[1], LANES), bf16),
            pltpu.VMEM((TALL, LANES), f32),
            pltpu.VMEM((dets, 2, FOLD, LANES), f32),
            pltpu.VMEM((dets, 2, 8, WIDE), f32),
            pltpu.VMEM((dets, 2, FOLD, WIDE), f32),
            pltpu.VMEM((slots, 2, FOLD, WIDE), f32),
            pltpu.VMEM((2, ROWS, COLS), bf16),
            pltpu.VMEM((COLS // 256, RADIX, 2 * FOLD, 256), f32),
            pltpu.VMEM((slots, ROWS, HALF), f32),
            pltpu.VMEM((slots, ROWS, HALF), f32),
            pltpu.VMEM((slots, 8, LANES), f32),
            pltpu.VMEM(first.shape, bf16),
            pltpu.VMEM(twiddle.shape, f32),
            pltpu.VMEM(second.shape, bf16),
            dma((5 + units,)),
            pltpu.SemaphoreType.REGULAR((bits,)),
            dma, dma((units,)),
            dma, dma((bits, units)),
            dma, dma((units, depth) if chain else (bits, units)),
            dma, dma((2, units, depth) if chain else (1,)),
            dma, dma((2, units)),
            dma, dma((slots, n)),
            dma((max(1, groups - 1),)), dma((slots, max(1, groups - 1))),
        ],
        compiler_params=pltpu.CompilerParams(
            collective_id=0, has_side_effects=True, vmem_limit_bytes=56 * 1024 * 1024
        ),
        name="search",
    )(
        lists.T, owner, cutoffs, slides, strain, bank,
        jnp.asarray(first), jnp.asarray(twiddle), jnp.asarray(second),
    )
    return results[:slots], results[slots:]


def solution(mesh):
    in_specs = (
        P(("grp", "tpl"), None, None, None),
        P(None, None, "tpl"),
        P(),
        P(),
        P("grp"),
        P("grp"),
    )
    out_specs = (P(("grp", "tpl")), P(("grp", "tpl")))
    width = len({d.coords[1] for d in mesh.devices[0].flat})
    body_of = functools.partial(body, width)
    return jax.shard_map(body_of, mesh=mesh, in_specs=in_specs, out_specs=out_specs, check_vma=False)
```
